32 devices in a mesh: frame: 8 (over y, x, core), tensor: 4 (over z).
Axes of the slice: x: 2, y: 2, z: 4, core: 2. Of those that a mesh axis runs over, the one named last changes fastest.
Arguments:
- tokens: bfloat16 [1024, 1, 4096], P(('frame', 'tensor')), may hold values from -6 to 6
- norm_gain: float32 [4096], replicated, may hold values from 0.5 to 1.5
- query_weight: bfloat16 [4096, 4096], P(None, 'tensor'), may hold values from -0.09375 to 0.09375
- out_weight: bfloat16 [4096, 4096], P('tensor'), may hold values from -0.09375 to 0.09375
- cache_keys: bfloat16 [384, 1, 4096], P('frame', None, 'tensor'), may hold values from -420 to 420
- cache_values: bfloat16 [384, 1, 4096], P('frame', None, 'tensor'), may hold values from -18 to 18
- token_pos: int32 [1024, 1], P('frame'), may hold values from 0 to 383, as said below
- frame_pad: int32 [1], replicated, may hold values from 0 to 192
Outputs:
- mixed: bfloat16 [1024, 1, 4096], P(('frame', 'tensor'))
The draws below stay inside these ranges and needn't reach their ends.
Inputs may be any that keep to these rules, and one draw needn't show every extreme that they name: `token_pos`: nondecreasing along each sequence; the last token of every sequence has 383.
All inputs are finite; a program needn't handle non-finite values.
Results may differ from the reference program's by a relative error of at most 0.018.
Values may be sent and summed in bfloat16 or wider, within the bound.
A program may use at most 64 MiB of HBM per device.

```python
import jax
import jax.numpy as jnp
from jax import lax

D = 4096
HEADS = 32
HEAD_DIM = 128
SEQS = 1
LENGTH = 1024
FRAMES = 384
N_TENSOR = 4


def draw_token_pos(key, part):
    climbs = jax.random.randint(jax.random.fold_in(key, 11), (LENGTH, SEQS), 0, 3)
    climbed = jnp.cumsum(climbs, axis=0)
    placed = jnp.minimum(climbed * FRAMES // LENGTH, FRAMES - 1)
    finals = jnp.arange(LENGTH)[:, None] == LENGTH - 1
    return jnp.where(finals, FRAMES - 1, placed).astype(jnp.int32)


def draw_cache_keys(key, part):
    shape = (FRAMES, SEQS, HEADS * HEAD_DIM)
    base = 2.0 * jax.random.normal(jax.random.fold_in(key, 23), shape, jnp.float32)
    return jnp.clip(base, -12.0, 12.0).astype(jnp.bfloat16)


def block_scale(stream_key, extent, shards, smallest, top_value):
    level, own = 1.0, jax.random.fold_in(stream_key, 6)
    for dim, blocks in shards:
        draws = jnp.exp(jax.random.uniform(jax.random.fold_in(own, dim), (blocks,), jnp.float32, smallest / len(shards), top_value / len(shards)))
        level = level * jnp.repeat(draws, extent[dim] // blocks).reshape([-1 if axis == dim else 1 for axis in range(len(extent))])
    return level


def bell_draw(key, dims, spread, bound, split=(), kind=jnp.bfloat16):
    drawn = spread * jax.random.normal(key, dims, jnp.float32)
    if split:
        drawn = drawn * block_scale(key, dims, split, -0.22, 0.18)
    return jnp.clip(drawn, -bound, bound).astype(kind)


def setup_inputs(seed: int = 0) -> dict:
    keys = jax.random.split(jax.random.key(seed), 9)
    tokens = bell_draw(keys[0], (LENGTH, SEQS, D), 1.0, 6.0, ((0, 32),))
    norm_gain = jnp.clip(1.0 + 0.1 * jax.random.normal(keys[1], (D,), jnp.float32), 0.5, 1.5)
    query_weight = bell_draw(keys[2], (D, HEADS * HEAD_DIM), D ** -0.5, 0.09375, ((1, 4),))
    out_weight = bell_draw(keys[3], (HEADS * HEAD_DIM, D), (HEADS * HEAD_DIM) ** -0.5, 0.09375, ((0, 4),))
    cache_keys = draw_cache_keys(jax.random.fold_in(keys[8], 71), 0)
    cache_values = bell_draw(keys[5], (FRAMES, SEQS, HEADS * HEAD_DIM), 3.0, 18.0, ((0, 8), (2, 4)))
    token_pos = draw_token_pos(jax.random.fold_in(keys[8], 71), 0)
    frame_pad = jax.random.randint(keys[7], (SEQS,), 0, FRAMES // 2 + 1).astype(jnp.int32)
    return {"tokens": tokens, "norm_gain": norm_gain, "query_weight": query_weight, "out_weight": out_weight, "cache_keys": cache_keys, "cache_values": cache_values, "token_pos": token_pos, "frame_pad": frame_pad}


epsilon = 1e-06
masked_score = -1e+30

def reference(tokens, norm_gain, query_weight, out_weight, cache_keys, cache_values, token_pos, frame_pad):
    hidden = tokens.astype(jnp.float32)
    factor = lax.rsqrt(lax.optimization_barrier(jnp.mean(hidden * hidden, axis=-1, keepdims=True)) + epsilon)
    normed = (hidden * factor * norm_gain.astype(jnp.float32)).astype(jnp.bfloat16)
    queries = (jnp.dot(normed, query_weight, preferred_element_type=jnp.float32) * HEAD_DIM ** (-0.5)).astype(jnp.bfloat16)
    frame_index = jnp.arange(FRAMES, dtype=jnp.int32)
    valid_frames = (FRAMES - frame_pad).astype(jnp.int32)
    visible = (frame_index[None, :, None] <= token_pos[:, None, :]) & (frame_index[None, :, None] < valid_frames[None, None, :])
    query_heads = queries.reshape(LENGTH, SEQS, HEADS, HEAD_DIM).transpose(2, 0, 1, 3)
    key_heads = cache_keys.reshape(FRAMES, SEQS, HEADS, HEAD_DIM).transpose(2, 0, 1, 3)
    value_heads = cache_values.reshape(FRAMES, SEQS, HEADS, HEAD_DIM).transpose(2, 0, 1, 3)

    def one_head(operands):
        query_one, key_one, value_one = operands
        scores = jnp.einsum('lsd,fsd->lfs', query_one.astype(jnp.float32), key_one.astype(jnp.float32))
        scores = jnp.where(visible, scores, masked_score)
        highest = lax.optimization_barrier(jnp.max(scores, axis=1, keepdims=True))
        weights = jnp.where(visible, jnp.exp(scores - highest), 0.0)
        summed = lax.optimization_barrier(jnp.sum(weights, axis=1))
        rounded = lax.optimization_barrier(weights.astype(jnp.bfloat16)).astype(jnp.float32)
        gathered = jnp.einsum('lfs,fsd->lsd', rounded, value_one.astype(jnp.float32))
        return (gathered / summed[:, :, None]).astype(jnp.bfloat16)
    attended = lax.map(one_head, (query_heads, key_heads, value_heads))
    per_group = HEADS // N_TENSOR
    groups = attended.reshape(N_TENSOR, per_group, LENGTH, SEQS, HEAD_DIM).transpose(0, 2, 3, 1, 4)
    groups = groups.reshape(N_TENSOR, LENGTH, SEQS, per_group * HEAD_DIM)
    weight_groups = out_weight.reshape(N_TENSOR, per_group * HEAD_DIM, D)

    def add_group(running, operands):
        head_group, weight_group = operands
        partial_value = jnp.dot(head_group, weight_group, preferred_element_type=jnp.float32)
        partial_value = lax.optimization_barrier(partial_value.astype(jnp.bfloat16)).astype(jnp.float32)
        return (running + partial_value, None)
    summed_out, _ = lax.scan(add_group, jnp.zeros((LENGTH, SEQS, D), jnp.float32), (groups, weight_groups))
    return summed_out.astype(jnp.bfloat16)
```

```python
import functools
import math

import jax
import jax.numpy as jnp
from jax import lax
from jax.experimental import pallas as pl
from jax.experimental.pallas import tpu as pltpu
from jax.sharding import PartitionSpec as P

HEAD_DIM = 128
epsilon = 1e-06
masked_score = -1e30
MESH = pl.DeviceIdType.MESH


def flip(index, bit):
    return index + bit - 2 * bit * lax.rem(lax.div(index, bit), 2)


def kernel(
    n, frames_n, x_tile, o_tile,
    tok, gain_hbm, wq_hbm, wo_hbm, keys, values, pos_hbm, pad,
    out,
    wq, wo, kg, vg, pos_col, gain, pos, raw, xg, qacc, qall, abuf, pbuf, rbuf, sums,
    q_sem, o_sem, own_sem, small_sem, kv_own, k_send, k_recv, v_send, v_recv,
    x_send, x_recv, p_send, p_recv,
):
    me_f = lax.axis_index("frame")
    me = lax.axis_index("tensor")
    rows = tok.shape[0]
    width = tok.shape[1]
    cols = wq.shape[1]
    span = keys.shape[0]
    bits = [1 << b for b in range(int(math.log2(frames_n)))][::-1]
    phase_n = len(bits)
    v_order = bits[1::-1] + bits[2:] if phase_n > 1 else bits
    n_x = width // x_tile
    n_out = width // o_tile
    lag = n_out // 2
    passed = 0
    has_left = me > 0
    has_right = me < n - 1
    middle = jnp.logical_and(has_left, has_right)
    low_half = 2 * me < n

    def q_load(part):
        window = pl.ds(pl.multiple_of(part * x_tile, x_tile), x_tile)
        return pltpu.make_async_copy(wq_hbm.at[window], wq.at[window], q_sem.at[part])

    def o_load(part):
        depth = cols // 2
        window = pl.ds(part * depth, depth)
        return pltpu.make_async_copy(wo_hbm.at[window], wo.at[window], o_sem.at[part])

    own_x = pltpu.make_async_copy(tok, raw, own_sem)
    own_k = pltpu.make_async_copy(keys, kg.at[pl.ds(0, span)], kv_own.at[0])
    own_v = pltpu.make_async_copy(values, vg.at[pl.ds(0, span)], kv_own.at[1])

    own_x.start()
    own_gain = pltpu.make_async_copy(gain_hbm, gain, small_sem.at[0])
    own_pos = pltpu.make_async_copy(pos_hbm, pos, small_sem.at[1])
    own_gain.start()
    own_pos.start()
    barrier = pltpu.get_barrier_semaphore()
    for bit in bits:
        pl.semaphore_signal(
            barrier, inc=1, device_id={"frame": flip(me_f, bit)}, device_id_type=MESH
        )

    @pl.when(has_left)
    def _():
        pl.semaphore_signal(barrier, inc=1, device_id={"tensor": me - 1}, device_id_type=MESH)

    @pl.when(has_right)
    def _():
        pl.semaphore_signal(barrier, inc=1, device_id={"tensor": me + 1}, device_id_type=MESH)

    @pl.when(jnp.logical_not(middle))
    def _():
        pl.semaphore_signal(
            barrier, inc=1, device_id={"tensor": n - 1 - me}, device_id_type=MESH
        )

    own_k.start()
    own_v.start()
    for part in range(n_x):
        q_load(part).start()
    for part in range(2):
        o_load(part).start()

    own_pos.wait()
    pos_col[...] = jnp.broadcast_to(pos[...], (HEAD_DIM, n * rows)).T
    own_x.wait()
    own_gain.wait()
    hidden = raw[...].astype(jnp.float32)
    factor = lax.rsqrt(jnp.mean(hidden * hidden, axis=-1, keepdims=True) + epsilon)
    xg[me] = (hidden * factor * gain[...]).astype(jnp.bfloat16)

    pl.semaphore_wait(barrier, phase_n + 2)

    def token_copy(block, side, chunk):
        towards = lax.rem(me + 1 - 2 * side + n, n)
        window = pl.ds(pl.multiple_of(chunk * x_tile, x_tile), x_tile)
        return pltpu.make_async_remote_copy(
            src_ref=xg.at[block, :, window],
            dst_ref=xg.at[block, :, window],
            send_sem=x_send.at[side, block, chunk],
            recv_sem=x_recv.at[block, chunk],
            device_id={"tensor": towards},
            device_id_type=MESH,
        )

    for chunk in range(n_x):
        @pl.when(has_right)
        def _():
            token_copy(me, 0, chunk).start()

        @pl.when(has_left)
        def _():
            token_copy(me, 1, chunk).start()

    def exchange(ref, source, send, recv, order, phase):
        bit = order[phase]
        held = [0]
        for earlier in order[:phase]:
            held = held + [slot + earlier for slot in held]
        copies = []
        for slot in held:
            src = source if slot == 0 else ref.at[pl.ds(slot * span, span)]
            copies.append(
                pltpu.make_async_remote_copy(
                    src_ref=src,
                    dst_ref=ref.at[pl.ds((slot + bit) * span, span)],
                    send_sem=send.at[slot + bit],
                    recv_sem=recv.at[slot + bit],
                    device_id={"frame": flip(me_f, bit)},
                    device_id_type=MESH,
                )
            )
        return copies

    phases = [
        exchange(kg, keys, k_send, k_recv, bits, p)
        + exchange(vg, values, v_send, v_recv, v_order, p)
        for p in range(phase_n)
    ]

    def begin(p):
        for copy in phases[p]:
            copy.start()

    def finish(p):
        for copy in phases[p]:
            copy.wait_recv()

    begin(0)

    slot_of = lax.broadcasted_iota(jnp.int32, (1, span), 1)
    pieces = []
    for slot in range(frames_n):
        owner = me_f
        for bit in bits:
            if slot & bit:
                owner = flip(owner, bit)
        pieces.append(slot_of + owner * span)
    frame_index = jnp.concatenate(pieces, axis=1)
    visible_frames = frame_index < frames_n * span - pad[0]

    def q_step(block, side, chunk):
        window = pl.ds(pl.multiple_of(chunk * x_tile, x_tile), x_tile)
        product = jnp.dot(xg[block, :, window], wq[window, :], preferred_element_type=jnp.float32)

        @pl.when(chunk == 0)
        def _():
            qacc[side] = product

        @pl.when(chunk > 0)
        def _():
            qacc[side] += product

        @pl.when(chunk == n_x - 1)
        def _():
            qall[block] = (qacc[side] * HEAD_DIM ** (-0.5)).astype(jnp.bfloat16)

    def own_body(chunk, _):
        q_load(chunk).wait()
        q_step(me, 0, chunk)
        return 0

    lax.fori_loop(0, n_x, own_body, 0)
    for p in range(1, phase_n - 1):
        finish(p - 1)
        begin(p)

    def part_copy(block, side, tile, far=False):
        towards = jnp.where(far, block, lax.rem(me + 1 - 2 * side + n, n))
        slot = jnp.where(far, 1 - side, side)
        window = pl.ds(pl.multiple_of(tile * o_tile, o_tile), o_tile)
        return pltpu.make_async_remote_copy(
            src_ref=pbuf.at[block, :, window],
            dst_ref=rbuf.at[slot, block, :, window],
            send_sem=p_send.at[block, tile],
            recv_sem=p_recv.at[slot, block, tile],
            device_id={"tensor": towards},
            device_id_type=MESH,
        )

    def send_part(block, side, tile, far):
        early = tile < passed
        held = jnp.logical_and(middle, early)

        @pl.when(jnp.logical_not(held))
        def _():
            part_copy(block, side, tile, jnp.logical_and(far, jnp.logical_not(early))).start()

    def attend(block, send, side, far):
        block_pos = pos_col[pl.ds(pl.multiple_of(block * rows, rows), rows), :1]
        visible = (frame_index <= block_pos) & visible_frames
        windows = [slice(i, i + HEAD_DIM) for i in range(0, cols, HEAD_DIM)]
        scores = [
            lax.dot_general(
                qall[block, :, window], kg[:, window], (((1,), (1,)), ((), ())),
                preferred_element_type=jnp.float32,
            )
            for window in windows
        ]
        scores = [jnp.where(visible, score, masked_score) for score in scores]
        highest = [jnp.max(score, axis=-1, keepdims=True) for score in scores]
        weights = [
            jnp.where(visible, jnp.exp(score - top), 0.0) for score, top in zip(scores, highest)
        ]
        totals = [jnp.sum(weight, axis=-1, keepdims=True) for weight in weights]
        gathered = [
            jnp.dot(weight.astype(jnp.bfloat16), vg[:, window], preferred_element_type=jnp.float32)
            for weight, window in zip(weights, windows)
        ]
        for window, value, total in zip(windows, gathered, totals):
            abuf[:, window] = (value / total).astype(jnp.bfloat16)

        def o_body(tile, _):
            window = pl.ds(pl.multiple_of(tile * o_tile, o_tile), o_tile)
            pbuf[block, :, window] = jnp.dot(
                abuf[...], wo[:, window], preferred_element_type=jnp.float32
            ).astype(jnp.bfloat16)
            @pl.when(jnp.logical_and(send, tile > 0))
            def _():
                send_part(block, side, tile - 1, far)

            return 0

        lax.fori_loop(0, n_out, o_body, 0)
        @pl.when(send)
        def _():
            send_part(block, side, n_out - 1, far)

    def stage_body(stage, _):
        before = me - stage
        after = me + stage

        def chunk_body(chunk, _):
            @pl.when(before >= 0)
            def _():
                token_copy(before, 0, chunk).wait_recv()

                @pl.when(has_right)
                def _():
                    token_copy(before, 0, chunk).start()

            @pl.when(after < n)
            def _():
                token_copy(after, 1, chunk).wait_recv()

                @pl.when(has_left)
                def _():
                    token_copy(after, 1, chunk).start()

            def side_body(side, _):
                block = me + (2 * side - 1) * stage

                @pl.when(jnp.logical_and(block >= 0, block < n))
                def _():
                    q_step(block, side, chunk)

                return 0

            lax.fori_loop(0, 2, side_body, 0)
            return 0

        lax.fori_loop(0, n_x, chunk_body, 0)

        @pl.when(stage == 1)
        def _():
            if phase_n > 1:
                finish(phase_n - 2)
                begin(phase_n - 1)
            finish(phase_n - 1)
            own_k.wait()
            own_v.wait()
            for part in range(2):
                o_load(part).wait()

        @pl.when(jnp.logical_or(jnp.logical_not(middle), stage == 1))
        def _():
            end_block = jnp.where(has_left, n - 1 - stage, stage)
            near_block = jnp.where(low_half, me + 1, me - 1)
            block = jnp.where(middle, near_block, end_block)
            ends = jnp.logical_not(middle)
            send = jnp.logical_or(ends, starts_sum(block))
            far = jnp.logical_and(ends, stage == n - 1)
            attend(block, send, jnp.where(block > me, 0, 1), far)

        return 0

    def starts_sum(block):
        up = jnp.logical_and(me == 1, block == n - 1)
        down = jnp.logical_and(me == n - 2, block == 0)
        return jnp.logical_or(up, down)

    lax.fori_loop(1, n, stage_body, 0)

    def relay_body(index, _):
        def side_body(turn, _):
            side = jnp.where(low_half, turn, 1 - turn)
            at = index - turn * lag
            known = jnp.logical_and(at >= 0, at < n * n_out)
            at = jnp.maximum(at, 0)
            stage = lax.div(at, n_out)
            tile = lax.rem(at, n_out)
            known = jnp.logical_and(known, jnp.logical_or(stage > 0, tile >= passed))
            known = jnp.logical_and(known, jnp.logical_or(stage < n - 1, tile < passed))
            stage = jnp.where(stage == 0, n - 1, stage)
            window = pl.ds(pl.multiple_of(tile * o_tile, o_tile), o_tile)
            block = jnp.where(side == 0, stage, n - 1 - stage)
            passes = jnp.where(side == 0, block > me, block < me)
            sent = jnp.logical_and(starts_sum(block), tile >= passed)
            passes = jnp.logical_and(passes, jnp.logical_not(sent))

            @pl.when(jnp.logical_and(known, passes))
            def _():
                part_copy(block, side, tile).wait_recv()
                pbuf[block, :, window] = (
                    pbuf[block, :, window].astype(jnp.float32)
                    + rbuf[side, block, :, window].astype(jnp.float32)
                ).astype(jnp.bfloat16)
                part_copy(block, side, tile).start()

            return 0

        lax.fori_loop(0, 2, side_body, 0)
        return 0

    def late_body(index, _):
        step = jnp.where(low_half, index, n - index)
        block = lax.rem(me + step, n)

        @pl.when(jnp.logical_and(middle, index == n))
        def _():
            lax.fori_loop(0, n * n_out + lag, relay_body, 0)

        @pl.when(jnp.logical_or(middle, index == n))
        def _():
            send = jnp.logical_and(middle, starts_sum(block))
            attend(block, send, jnp.where(block > me, 0, 1), False)

        return 0

    lax.fori_loop(2, n + 1, late_body, 0)

    def sum_body(tile, _):
        window = pl.ds(pl.multiple_of(tile * o_tile, o_tile), o_tile)

        sums[...] = pbuf[me, :, window].astype(jnp.float32)
        for side in range(2):
            from_far = jnp.logical_not(has_right if side else has_left)
            comes = jnp.logical_not(jnp.logical_and(from_far, tile < passed))

            @pl.when(comes)
            def _():
                part_copy(me, side, tile).wait_recv()
                sums[...] += rbuf[side, me, :, window].astype(jnp.float32)

        out[:, window] = sums[...].astype(jnp.bfloat16)
        return 0

    lax.fori_loop(0, n_out, sum_body, 0)

    def drain_body(block, _):
        for tile in range(n_out):
            @pl.when(block != me)
            def _():
                part_copy(block, 0, tile).wait_send()

        for chunk in range(n_x):
            @pl.when(jnp.logical_and(has_right, block <= me))
            def _():
                token_copy(block, 0, chunk).wait_send()

            @pl.when(jnp.logical_and(has_left, block >= me))
            def _():
                token_copy(block, 1, chunk).wait_send()

        return 0

    lax.fori_loop(0, n, drain_body, 0)
    for group in phases:
        for copy in group:
            copy.wait_send()


def divisor(total, most):
    return math.gcd(total, most)


def per_device(
    n, frames_n,
    tokens, norm_gain, query_weight, out_weight, cache_keys, cache_values, token_pos, frame_pad
):
    rows, seqs, width = tokens.shape
    cols = query_weight.shape[1]
    span = cache_keys.shape[0]
    x_tile = divisor(width, 1024)
    o_tile = divisor(width, 1024)
    n_x = width // x_tile
    n_out = width // o_tile
    hbm = pl.BlockSpec(memory_space=pltpu.HBM)
    vmem = pl.BlockSpec(memory_space=pltpu.VMEM)
    bf16 = jnp.bfloat16
    dma = pltpu.SemaphoreType.DMA
    result = pl.pallas_call(
        functools.partial(kernel, n, frames_n, x_tile, o_tile),
        out_shape=pltpu.VMEM((rows, width), bf16),
        in_specs=[hbm, hbm, hbm, hbm, hbm, hbm, hbm, pl.BlockSpec(memory_space=pltpu.SMEM)],
        out_specs=vmem,
        scratch_shapes=[
            pltpu.VMEM(query_weight.shape, bf16),
            pltpu.VMEM(out_weight.shape, bf16),
            pltpu.VMEM((frames_n * span, cols), bf16),
            pltpu.VMEM((frames_n * span, cols), bf16),
            pltpu.VMEM((n * rows, HEAD_DIM), jnp.int32),
            pltpu.VMEM((1, width), jnp.float32),
            pltpu.VMEM((1, n * rows), jnp.int32),
            pltpu.VMEM((rows, width), bf16),
            pltpu.VMEM((n, rows, width), bf16),
            pltpu.VMEM((2, rows, cols), jnp.float32),
            pltpu.VMEM((n, rows, cols), bf16),
            pltpu.VMEM((rows, cols), bf16),
            pltpu.VMEM((n, rows, width), bf16),
            pltpu.VMEM((2, n, rows, width), bf16),
            pltpu.VMEM((rows, o_tile), jnp.float32),
            dma((n_x,)),
            dma((2,)),
            dma(()),
            dma((2,)),
            dma((2,)),
            dma((frames_n,)),
            dma((frames_n,)),
            dma((frames_n,)),
            dma((frames_n,)),
            dma((2, n, n_x)),
            dma((n, n_x)),
            dma((n, n_out)),
            dma((2, n, n_out)),
        ],
        compiler_params=pltpu.CompilerParams(collective_id=0, has_side_effects=True),
    )(
        tokens.reshape(rows, width),
        norm_gain.reshape(1, width),
        query_weight,
        out_weight,
        cache_keys.reshape(span, cols),
        cache_values.reshape(span, cols),
        token_pos.reshape(1, n * rows),
        frame_pad,
    )
    return result.reshape(rows, seqs, width)


def solution(mesh):
    placed = (
        P(("frame", "tensor"), None, None),
        P(),
        P(None, "tensor"),
        P("tensor", None),
        P("frame", None, "tensor"),
        P("frame", None, "tensor"),
        P("frame", None),
        P(),
    )
    return jax.shard_map(
        functools.partial(per_device, mesh.shape["tensor"], mesh.shape["frame"]),
        mesh=mesh,
        in_specs=placed,
        out_specs=P(("frame", "tensor"), None, None),
        check_vma=False,
    )
```

```python
import functools
import math

import jax
import jax.numpy as jnp
from jax import lax
from jax.experimental import pallas as pl
from jax.experimental.pallas import tpu as pltpu
from jax.sharding import PartitionSpec as P

HEAD_DIM = 128
epsilon = 1e-06
masked_score = -1e30
MESH = pl.DeviceIdType.MESH


def flip(index, bit):
    return index + bit - 2 * bit * lax.rem(lax.div(index, bit), 2)


def kernel(
    n, frames_n, x_tile, o_tile, p_tile, lag, direct, early,
    tok, gain_hbm, wq_hbm, wo_hbm, keys, values, pos_hbm, pad,
    out,
    wq, wo, kg, vg, pos_col, gain, pos, raw, xg, qacc, qall, abuf, pbuf, rbuf,
    q_sem, o_sem, own_sem, small_sem, kv_own, k_send, k_recv, v_send, v_recv,
    x_send, x_recv, p_send, p_recv,
):
    me_f = lax.axis_index("frame")
    me = lax.axis_index("tensor")
    rows = tok.shape[0]
    width = tok.shape[1]
    cols = wq.shape[1]
    span = keys.shape[0]
    bits = [1 << b for b in range(int(math.log2(frames_n)))][::-1]
    phase_n = len(bits)
    k_order = bits
    v_order = bits[1::-1] + bits[2:] if phase_n > 1 else bits
    n_x = width // x_tile
    n_out = width // o_tile
    n_part = width // p_tile
    per_out = o_tile // p_tile
    chained = n_part - direct
    has_left = me > 0
    has_right = me < n - 1
    middle = jnp.logical_and(has_left, has_right)
    low_half = 2 * me < n

    def q_load(part):
        window = pl.ds(part * x_tile, x_tile)
        return pltpu.make_async_copy(wq_hbm.at[window], wq.at[window], q_sem.at[part])

    def o_load(part):
        depth = cols // 2
        window = pl.ds(part * depth, depth)
        return pltpu.make_async_copy(wo_hbm.at[window], wo.at[window], o_sem.at[part])

    def rows_of(block, count=1):
        return pl.ds(pl.multiple_of(block * rows, rows), count * rows)

    own_x = pltpu.make_async_copy(tok, raw, own_sem)
    own_gain = pltpu.make_async_copy(gain_hbm, gain, small_sem.at[0])
    own_pos = pltpu.make_async_copy(pos_hbm, pos, small_sem.at[1])
    own_k = pltpu.make_async_copy(keys, kg.at[pl.ds(0, span)], kv_own.at[0])
    own_v = pltpu.make_async_copy(values, vg.at[pl.ds(0, span)], kv_own.at[1])

    barrier = pltpu.get_barrier_semaphore()
    for bit in bits:
        pl.semaphore_signal(
            barrier, inc=1, device_id={"frame": flip(me_f, bit)}, device_id_type=MESH
        )

    @pl.when(has_left)
    def _():
        pl.semaphore_signal(barrier, inc=1, device_id={"tensor": me - 1}, device_id_type=MESH)

    @pl.when(has_right)
    def _():
        pl.semaphore_signal(barrier, inc=1, device_id={"tensor": me + 1}, device_id_type=MESH)

    own_x.start()
    own_gain.start()
    own_pos.start()
    own_k.start()
    own_v.start()

    own_x.wait()
    own_gain.wait()
    own_k.wait()
    own_v.wait()
    for part in range(n_x):
        q_load(part).start()
    for part in range(2):
        o_load(part).start()
    hidden = raw[...].astype(jnp.float32)
    factor = lax.rsqrt(jnp.mean(hidden * hidden, axis=-1, keepdims=True) + epsilon)
    xg[rows_of(me), :] = (hidden * factor * gain[...]).astype(jnp.bfloat16)
    own_pos.wait()
    pos_col[...] = jnp.broadcast_to(pos[...], (HEAD_DIM, n * rows)).T

    pl.semaphore_wait(
        barrier, phase_n + has_left.astype(jnp.int32) + has_right.astype(jnp.int32)
    )

    def neighbour(side):
        return lax.rem(me + 1 - 2 * side + n, n)

    def token_copy(block, side, chunk):
        window = pl.ds(chunk * x_tile, x_tile)
        if not isinstance(chunk, int):
            window = pl.ds(pl.multiple_of(chunk * x_tile, x_tile), x_tile)
        return pltpu.make_async_remote_copy(
            src_ref=xg.at[rows_of(block), window],
            dst_ref=xg.at[rows_of(block), window],
            send_sem=x_send.at[side, block, chunk],
            recv_sem=x_recv.at[block, chunk],
            device_id={"tensor": neighbour(side)},
            device_id_type=MESH,
        )

    for chunk in range(n_x):
        @pl.when(has_right)
        def _():
            token_copy(me, 0, chunk).start()

        @pl.when(has_left)
        def _():
            token_copy(me, 1, chunk).start()

    def frame_copy(ref, slot, bit, send, recv):
        return pltpu.make_async_remote_copy(
            src_ref=ref.at[pl.ds(slot * span, span)],
            dst_ref=ref.at[pl.ds((slot + bit) * span, span)],
            send_sem=send.at[slot + bit],
            recv_sem=recv.at[slot + bit],
            device_id={"frame": flip(me_f, bit)},
            device_id_type=MESH,
        )

    def plan(ref, order, send, recv):
        steps, held = [], [0]
        for p, bit in enumerate(order):
            fresh = [slot + bit for slot in held]
            for slot in fresh:
                arrival = frame_copy(ref, slot - bit, bit, send, recv)
                onward = [frame_copy(ref, slot, later, send, recv) for later in order[p + 1:]]
                steps.append((arrival, onward))
            held = held + fresh
        own = [frame_copy(ref, 0, bit, send, recv) for bit in order]
        return own, steps

    k_own, k_steps = plan(kg, k_order, k_send, k_recv)
    v_own, v_steps = plan(vg, v_order, v_send, v_recv)
    for pair in zip(k_own, v_own):
        for copy in pair:
            copy.start()
    relays = [pair for pair in zip(k_steps, v_steps) if pair[0][1]]
    last_ones = [pair for pair in zip(k_steps, v_steps) if not pair[0][1]]

    def frame_step(pair):
        for arrival, onward in pair:
            arrival.wait_recv()
            for copy in onward:
                copy.start()

    def frame_steps(chunk):
        if chunk < n_x - 2:
            for pair in relays[chunk:chunk + 1]:
                frame_step(pair)
        if chunk == n_x - 1:
            for pair in relays[max(n_x - 2, 0):]:
                frame_step(pair)

    def frames_done():
        for pair in last_ones:
            frame_step(pair)

    slot_of = lax.broadcasted_iota(jnp.int32, (1, span), 1)
    pieces = []
    for slot in range(frames_n):
        owner = me_f
        for bit in bits:
            if slot & bit:
                owner = flip(owner, bit)
        pieces.append(slot_of + owner * span)
    frame_index = jnp.concatenate(pieces, axis=1)
    visible_frames = frame_index < frames_n * span - pad[0]

    scale = HEAD_DIM ** (-0.5)

    def q_first(block, count, chunk):
        window = slice(chunk * x_tile, (chunk + 1) * x_tile)
        at = rows_of(block, count)
        held = pl.ds(0, count * rows)
        product = jnp.dot(xg[at, window], wq[window, :], preferred_element_type=jnp.float32)
        if chunk > 0:
            product = qacc[held, :] + product
        if chunk < n_x - 1:
            qacc[held, :] = product
        else:
            qall[at, :] = (product * scale).astype(jnp.bfloat16)

    def q_step(block, place, chunk):
        window = pl.ds(pl.multiple_of(chunk * x_tile, x_tile), x_tile)
        held = pl.ds(place * rows, rows)
        if not isinstance(place, int):
            held = rows_of(place)
        product = jnp.dot(
            xg[rows_of(block), window], wq[window, :], preferred_element_type=jnp.float32
        )

        @pl.when(chunk == 0)
        def _():
            qacc[held, :] = product

        @pl.when(chunk > 0)
        def _():
            qacc[held, :] += product

        @pl.when(chunk == n_x - 1)
        def _():
            qall[rows_of(block), :] = (qacc[held, :] * scale).astype(jnp.bfloat16)

    def attend(block, count):
        at = rows_of(block, count)
        visible = (frame_index <= pos_col[at, :1]) & visible_frames
        windows = [slice(i, i + HEAD_DIM) for i in range(0, cols, HEAD_DIM)]
        scores = [
            lax.dot_general(
                qall[at, window], kg[:, window], (((1,), (1,)), ((), ())),
                preferred_element_type=jnp.float32,
            )
            for window in windows
        ]
        scores = [jnp.where(visible, score, masked_score) for score in scores]
        highest = [jnp.max(score, axis=-1, keepdims=True) for score in scores]
        weights = [
            jnp.where(visible, jnp.exp(score - top), 0.0) for score, top in zip(scores, highest)
        ]
        totals = [jnp.sum(weight, axis=-1, keepdims=True) for weight in weights]
        gathered = [
            jnp.dot(weight.astype(jnp.bfloat16), vg[:, window], preferred_element_type=jnp.float32)
            for weight, window in zip(weights, windows)
        ]
        for window, value, total in zip(windows, gathered, totals):
            abuf[at, window] = (value / total).astype(jnp.bfloat16)

    def part_window(tile):
        return pl.ds(pl.multiple_of(tile * p_tile, p_tile), p_tile)

    def part_copy(block, side, tile, far=False):
        slot = jnp.where(far, 1 - side, side)
        towards = jnp.where(far, block, neighbour(side))
        return pltpu.make_async_remote_copy(
            src_ref=pbuf.at[rows_of(block), part_window(tile)],
            dst_ref=rbuf.at[slot, rows_of(block), part_window(tile)],
            send_sem=p_send.at[block, tile],
            recv_sem=p_recv.at[slot, block, tile],
            device_id={"tensor": towards},
            device_id_type=MESH,
        )

    def project(block, count, first_tile, send):
        at = rows_of(block, count)

        def body(index, _):
            tile = lax.rem(index + first_tile, n_out)
            window = pl.ds(pl.multiple_of(tile * o_tile, o_tile), o_tile)
            pbuf[at, window] = jnp.dot(
                abuf[at, :], wo[:, window], preferred_element_type=jnp.float32
            ).astype(jnp.bfloat16)

            @pl.when(index > 0)
            def _():
                send(lax.rem(tile + n_out - 1, n_out))

            return 0

        lax.fori_loop(0, n_out, body, 0)
        send((first_tile + n_out - 1) % n_out)

    def parts_of(tile):
        return [tile * per_out + part for part in range(per_out)]

    def drain_inputs():
        def drain_body(block, _):
            for chunk in range(n_x):
                @pl.when(jnp.logical_and(has_right, block <= me))
                def _():
                    token_copy(block, 0, chunk).wait_send()

                @pl.when(jnp.logical_and(has_left, block >= me))
                def _():
                    token_copy(block, 1, chunk).wait_send()

            return 0

        lax.fori_loop(0, n, drain_body, 0)
        for own, steps in ((k_own, k_steps), (v_own, v_steps)):
            for copy in own:
                copy.wait_send()
            for _, onward in steps:
                for copy in onward:
                    copy.wait_send()

    @pl.when(jnp.logical_not(middle))
    def _():
        heading = jnp.where(has_left, -1, 1)
        arriving = jnp.where(has_left, 0, 1)
        leaving = 1 - arriving
        near = me + heading
        first = jnp.minimum(me, near)
        for chunk in range(n_x):
            q_load(chunk).wait()
            token_copy(near, arriving, chunk).wait_recv()
            q_first(first, 2, chunk)
            frame_steps(chunk)
        frames_done()
        attend(first, 2)
        for part in range(2):
            o_load(part).wait()


        def send_near(tile):
            for part in parts_of(tile):
                part_copy(near, leaving, part).start()

        project(first, 2, 0, send_near)

        def stage_body(stage, _):
            block = me + heading * stage

            def chunk_body(chunk, _):
                token_copy(block, arriving, chunk).wait_recv()
                q_step(block, 0, chunk)
                return 0

            lax.fori_loop(0, n_x, chunk_body, 0)
            attend(block, 1)

            def send_block(tile):
                for part in parts_of(tile):
                    far = jnp.logical_and(stage == n - 1, part >= chained)
                    part_copy(block, leaving, part, far).start()

            project(block, 1, 0, send_block)
            return 0

        lax.fori_loop(2, n, stage_body, 0)
        drain_inputs()

        def sum_body(tile, _):
            window = part_window(tile)
            part_copy(me, arriving, tile).wait_recv()
            total = pbuf[rows_of(me), window].astype(jnp.float32)
            total = total + rbuf[arriving, rows_of(me), window].astype(jnp.float32)

            @pl.when(tile < chained)
            def _():
                out[:, window] = total.astype(jnp.bfloat16)

            @pl.when(tile >= chained)
            def _():
                part_copy(me, leaving, tile).wait_recv()
                straight = rbuf[leaving, rows_of(me), window].astype(jnp.float32)
                out[:, window] = (total + straight).astype(jnp.bfloat16)

            return 0

        def sum_index(index, _):
            return sum_body(lax.rem(index + chained, n_part), 0)

        lax.fori_loop(0, n_part, sum_index, 0)

    @pl.when(middle)
    def _():
        for chunk in range(n_x):
            q_load(chunk).wait()
            for side, block in ((0, me - 1), (1, me + 1)):
                token_copy(block, side, chunk).wait_recv()
                token_copy(block, side, chunk).start()
            q_first(me - 1, 3, chunk)
            frame_steps(chunk)

        def stage_body(stage, _):
            def chunk_body(chunk, _):
                def side_body(side, _):
                    block = me - stage + 2 * side * stage

                    @pl.when(jnp.logical_and(block >= 0, block < n))
                    def _():
                        token_copy(block, side, chunk).wait_recv()
                        token_copy(block, side, chunk).start()
                        q_step(block, side, chunk)

                    return 0

                lax.fori_loop(0, 2, side_body, 0)
                return 0

            lax.fori_loop(0, n_x, chunk_body, 0)
            return 0

        lax.fori_loop(2, n - 1, stage_body, 0)
        frames_done()
        groups = max(1, n * rows // HEAD_DIM)
        while n % groups:
            groups -= 1
        count = n // groups
        for part in range(2):
            o_load(part).wait()

        def group_body(group, _):
            attend(group * count, count)

            def send_started(tile):
                last = group == groups - 1
                for part in parts_of(tile):
                    @pl.when((me == 1) & last & (part >= chained))
                    def _():
                        part_copy(n - 1, 0, part).start()

                    @pl.when((me == n - 2) & (group == 0) & (part >= chained))
                    def _():
                        part_copy(0, 1, part).start()

            project(group * count, count, chained // per_out % n_out, send_started)
            return 0

        lax.fori_loop(0, groups, group_body, 0)

        def relay(block, side, tile):
            at = rows_of(block)
            window = part_window(tile)
            part_copy(block, side, tile).wait_recv()
            pbuf[at, window] = (
                pbuf[at, window].astype(jnp.float32)
                + rbuf[side, at, window].astype(jnp.float32)
            ).astype(jnp.bfloat16)
            part_copy(block, side, tile).start()

        def relay_body(index, _):
            def side_body(turn, _):
                side = jnp.where(low_half, turn, 1 - turn)
                at = index - turn * lag
                stage = 1 + lax.div(jnp.maximum(at, 0), n_part)
                tile = lax.rem(jnp.maximum(at, 0), n_part)
                block = jnp.where(side == 0, stage, n - 1 - stage)
                passes = jnp.where(side == 0, block > me, block < me)
                chain = (stage < n - 1) | ((stage == n - 1) & (tile < chained))

                @pl.when((at >= 0) & chain & passes)
                def _():
                    relay(block, side, tile)

                far = index - (n - 3) * n_part - early
                beside = jnp.where(side == 0, me == 1, me == n - 2)

                @pl.when((far >= 0) & (far < direct) & jnp.logical_not(beside))
                def _():
                    relay(jnp.where(side == 0, n - 1, 0), side, chained + far)

                return 0

            lax.fori_loop(0, 2, side_body, 0)
            return 0

        behind = jnp.minimum(me, n - 1 - me) * n_part
        lax.fori_loop(jnp.minimum(behind, (n - 3) * n_part), (n - 1) * n_part + lag, relay_body, 0)

        def sum_body(tile, _):
            window = part_window(tile)
            total = pbuf[rows_of(me), window].astype(jnp.float32)
            for side in range(2):
                part_copy(me, side, tile).wait_recv()
                total = total + rbuf[side, rows_of(me), window].astype(jnp.float32)
            out[:, window] = total.astype(jnp.bfloat16)
            return 0

        lax.fori_loop(0, n_part, sum_body, 0)
        drain_inputs()

    def drain_body(block, _):
        @pl.when(block != me)
        def _():
            for tile in range(n_part):
                part_copy(block, 0, tile).wait_send()

        return 0

    lax.fori_loop(0, n, drain_body, 0)


def divisor(total, most):
    return math.gcd(total, most)


def per_device(
    n, frames_n,
    tokens, norm_gain, query_weight, out_weight, cache_keys, cache_values, token_pos, frame_pad
):
    rows, seqs, width = tokens.shape
    cols = query_weight.shape[1]
    span = cache_keys.shape[0]
    x_tile = divisor(width, 1024)
    o_tile = divisor(width, 512)
    p_tile = divisor(o_tile, 256)
    n_x = width // x_tile
    n_part = width // p_tile
    lag = max(1, 5 * n_part // 8)
    direct = n_part if n > 2 else 0
    early = n_part // 4
    hbm = pl.BlockSpec(memory_space=pltpu.HBM)
    vmem = pl.BlockSpec(memory_space=pltpu.VMEM)
    bf16 = jnp.bfloat16
    dma = pltpu.SemaphoreType.DMA
    result = pl.pallas_call(
        functools.partial(kernel, n, frames_n, x_tile, o_tile, p_tile, lag, direct, early),
        out_shape=pltpu.VMEM((rows, width), bf16),
        in_specs=[hbm, hbm, hbm, hbm, hbm, hbm, hbm, pl.BlockSpec(memory_space=pltpu.SMEM)],
        out_specs=vmem,
        scratch_shapes=[
            pltpu.VMEM(query_weight.shape, bf16),
            pltpu.VMEM(out_weight.shape, bf16),
            pltpu.VMEM((frames_n * span, cols), bf16),
            pltpu.VMEM((frames_n * span, cols), bf16),
            pltpu.VMEM((n * rows, HEAD_DIM), jnp.int32),
            pltpu.VMEM((1, width), jnp.float32),
            pltpu.VMEM((1, n * rows), jnp.int32),
            pltpu.VMEM((rows, width), bf16),
            pltpu.VMEM((n * rows, width), bf16),
            pltpu.VMEM((3 * rows, cols), jnp.float32),
            pltpu.VMEM((n * rows, cols), bf16),
            pltpu.VMEM((n * rows, cols), bf16),
            pltpu.VMEM((n * rows, width), bf16),
            pltpu.VMEM((2, n * rows, width), bf16),
            dma((n_x,)),
            dma((2,)),
            dma(()),
            dma((2,)),
            dma((2,)),
            dma((frames_n,)),
            dma((frames_n,)),
            dma((frames_n,)),
            dma((frames_n,)),
            dma((2, n, n_x)),
            dma((n, n_x)),
            dma((n, n_part)),
            dma((2, n, n_part)),
        ],
        compiler_params=pltpu.CompilerParams(collective_id=0, has_side_effects=True),
    )(
        tokens.reshape(rows, width),
        norm_gain.reshape(1, width),
        query_weight,
        out_weight,
        cache_keys.reshape(span, cols),
        cache_values.reshape(span, cols),
        token_pos.reshape(1, n * rows),
        frame_pad,
    )
    return result.reshape(rows, seqs, width)


def solution(mesh):
    placed = (
        P(("frame", "tensor"), None, None),
        P(),
        P(None, "tensor"),
        P("tensor", None),
        P("frame", None, "tensor"),
        P("frame", None, "tensor"),
        P("frame", None),
        P(),
    )
    return jax.shard_map(
        functools.partial(per_device, mesh.shape["tensor"], mesh.shape["frame"]),
        mesh=mesh,
        in_specs=placed,
        out_specs=P(("frame", "tensor"), None, None),
        check_vma=False,
    )
```

```python
import functools
import math

import jax
import jax.numpy as jnp
from jax import lax
from jax.experimental import pallas as pl
from jax.experimental.pallas import tpu as pltpu
from jax.sharding import PartitionSpec as P

HEAD_DIM = 128
epsilon = 1e-06
masked_score = -1e30
MESH = pl.DeviceIdType.MESH


def flip(index, bit):
    return index + bit - 2 * bit * lax.rem(lax.div(index, bit), 2)


def kernel(
    n, frames_n, x_tile, o_tile, p_tile, lag, direct, early,
    tok, gain_hbm, wq_hbm, wo_hbm, keys, values, pos_hbm, pad,
    out,
    wq, wo, kg, vg, pos_col, gain, pos, raw, xg, qacc, qall, abuf, pbuf, rbuf,
    q_sem, o_sem, own_sem, small_sem, kv_own, k_send, k_recv, v_send, v_recv,
    x_send, x_recv, p_send, p_recv,
):
    me_f = lax.axis_index("frame")
    me = lax.axis_index("tensor")
    rows = tok.shape[0]
    width = tok.shape[1]
    cols = wq.shape[1]
    span = keys.shape[0]
    bits = [1 << b for b in range(int(math.log2(frames_n)))][::-1]
    phase_n = len(bits)
    k_order = bits
    v_order = bits[1::-1] + bits[2:] if phase_n > 1 else bits
    n_x = width // x_tile
    n_out = width // o_tile
    n_part = width // p_tile
    per_out = o_tile // p_tile
    chained = n_part - direct
    has_left = me > 0
    has_right = me < n - 1
    middle = jnp.logical_and(has_left, has_right)
    low_half = 2 * me < n

    def q_load(part):
        window = pl.ds(part * x_tile, x_tile)
        return pltpu.make_async_copy(wq_hbm.at[window], wq.at[window], q_sem.at[part])

    def o_load(part):
        depth = cols // 2
        window = pl.ds(part * depth, depth)
        return pltpu.make_async_copy(wo_hbm.at[window], wo.at[window], o_sem.at[part])

    def rows_of(block, count=1):
        return pl.ds(pl.multiple_of(block * rows, rows), count * rows)

    own_x = pltpu.make_async_copy(tok, raw, own_sem)
    own_gain = pltpu.make_async_copy(gain_hbm, gain, small_sem.at[0])
    own_pos = pltpu.make_async_copy(pos_hbm, pos, small_sem.at[1])
    own_k = pltpu.make_async_copy(keys, kg.at[pl.ds(0, span)], kv_own.at[0])
    own_v = pltpu.make_async_copy(values, vg.at[pl.ds(0, span)], kv_own.at[1])

    barrier = pltpu.get_barrier_semaphore()
    for bit in bits:
        pl.semaphore_signal(
            barrier, inc=1, device_id={"frame": flip(me_f, bit)}, device_id_type=MESH
        )

    @pl.when(has_left)
    def _():
        pl.semaphore_signal(barrier, inc=1, device_id={"tensor": me - 1}, device_id_type=MESH)

    @pl.when(has_right)
    def _():
        pl.semaphore_signal(barrier, inc=1, device_id={"tensor": me + 1}, device_id_type=MESH)

    own_x.start()
    own_gain.start()
    own_pos.start()
    own_k.start()
    own_v.start()

    own_x.wait()
    own_gain.wait()
    own_k.wait()
    own_v.wait()
    for part in range(n_x):
        q_load(part).start()
    for part in range(2):
        o_load(part).start()
    hidden = raw[...].astype(jnp.float32)
    factor = lax.rsqrt(jnp.mean(hidden * hidden, axis=-1, keepdims=True) + epsilon)
    xg[rows_of(me), :] = (hidden * factor * gain[...]).astype(jnp.bfloat16)
    own_pos.wait()
    pos_col[...] = jnp.broadcast_to(pos[...], (HEAD_DIM, n * rows)).T

    pl.semaphore_wait(
        barrier, phase_n + has_left.astype(jnp.int32) + has_right.astype(jnp.int32)
    )

    def neighbour(side):
        return lax.rem(me + 1 - 2 * side + n, n)

    def token_copy(block, side, chunk):
        window = pl.ds(chunk * x_tile, x_tile)
        if not isinstance(chunk, int):
            window = pl.ds(pl.multiple_of(chunk * x_tile, x_tile), x_tile)
        return pltpu.make_async_remote_copy(
            src_ref=xg.at[rows_of(block), window],
            dst_ref=xg.at[rows_of(block), window],
            send_sem=x_send.at[side, block],
            recv_sem=x_recv.at[block, chunk],
            device_id={"tensor": neighbour(side)},
            device_id_type=MESH,
        )

    for chunk in range(n_x):
        @pl.when(has_right)
        def _():
            token_copy(me, 0, chunk).start()

        @pl.when(has_left)
        def _():
            token_copy(me, 1, chunk).start()

    def frame_copy(ref, slot, bit, last, send, recv):
        target = slot + bit
        index = 0 if target & last else target % last + target // (2 * last) * last
        return pltpu.make_async_remote_copy(
            src_ref=ref.at[pl.ds(slot * span, span)],
            dst_ref=ref.at[pl.ds(target * span, span)],
            send_sem=send,
            recv_sem=recv.at[index],
            device_id={"frame": flip(me_f, bit)},
            device_id_type=MESH,
        )

    def plan(ref, order, send, recv):
        steps, held = [], [0]
        last = order[-1]
        for p, bit in enumerate(order[:-1]):
            fresh = [slot + bit for slot in held]
            for slot in fresh:
                arrival = frame_copy(ref, slot - bit, bit, last, send, recv)
                onward = [
                    frame_copy(ref, slot, later, last, send, recv) for later in order[p + 1:]
                ]
                steps.append((arrival, onward))
            held = held + fresh
        own = [frame_copy(ref, 0, bit, last, send, recv) for bit in order]
        half = pl.ds(0, len(held) * span)
        rest = pltpu.make_async_remote_copy(
            src_ref=ref.at[half],
            dst_ref=ref.at[half],
            send_sem=send,
            recv_sem=recv.at[0],
            device_id={"frame": flip(me_f, last)},
            device_id_type=MESH,
        )
        return own, steps, rest

    k_own, k_steps, k_rest = plan(kg, k_order, k_send, k_recv)
    v_own, v_steps, v_rest = plan(vg, v_order, v_send, v_recv)
    for pair in zip(k_own, v_own):
        for copy in pair:
            copy.start()
    relays = list(zip(k_steps, v_steps))

    def frame_step(pair):
        for arrival, onward in pair:
            arrival.wait_recv()
            for copy in onward:
                copy.start()

    def frame_steps(chunk):
        if chunk < n_x - 2:
            for pair in relays[chunk:chunk + 1]:
                frame_step(pair)
        if chunk == n_x - 1:
            for pair in relays[max(n_x - 2, 0):]:
                frame_step(pair)

    def frames_done():
        k_rest.wait_recv()
        v_rest.wait_recv()

    slot_of = lax.broadcasted_iota(jnp.int32, (1, span), 1)
    pieces = []
    for slot in range(frames_n):
        owner = me_f
        for bit in bits:
            if slot & bit:
                owner = flip(owner, bit)
        pieces.append(slot_of + owner * span)
    frame_index = jnp.concatenate(pieces, axis=1)
    visible_frames = frame_index < frames_n * span - pad[0]

    scale = HEAD_DIM ** (-0.5)

    def q_first(block, count, chunk):
        window = slice(chunk * x_tile, (chunk + 1) * x_tile)
        at = rows_of(block, count)
        held = pl.ds(0, count * rows)
        product = jnp.dot(xg[at, window], wq[window, :], preferred_element_type=jnp.float32)
        if chunk > 0:
            product = qacc[held, :] + product
        if chunk < n_x - 1:
            qacc[held, :] = product
        else:
            qall[at, :] = (product * scale).astype(jnp.bfloat16)

    def q_step(block, place, chunk):
        window = pl.ds(pl.multiple_of(chunk * x_tile, x_tile), x_tile)
        held = pl.ds(place * rows, rows)
        if not isinstance(place, int):
            held = rows_of(place)
        product = jnp.dot(
            xg[rows_of(block), window], wq[window, :], preferred_element_type=jnp.float32
        )

        @pl.when(chunk == 0)
        def _():
            qacc[held, :] = product

        @pl.when(chunk > 0)
        def _():
            qacc[held, :] += product

        @pl.when(chunk == n_x - 1)
        def _():
            qall[rows_of(block), :] = (qacc[held, :] * scale).astype(jnp.bfloat16)

    def attend(block, count):
        at = rows_of(block, count)
        visible = (frame_index <= pos_col[at, :1]) & visible_frames
        windows = [slice(i, i + HEAD_DIM) for i in range(0, cols, HEAD_DIM)]
        scores = [
            lax.dot_general(
                qall[at, window], kg[:, window], (((1,), (1,)), ((), ())),
                preferred_element_type=jnp.float32,
            )
            for window in windows
        ]
        scores = [jnp.where(visible, score, masked_score) for score in scores]
        highest = [jnp.max(score, axis=-1, keepdims=True) for score in scores]
        weights = [
            jnp.where(visible, jnp.exp(score - top), 0.0) for score, top in zip(scores, highest)
        ]
        totals = [jnp.sum(weight, axis=-1, keepdims=True) for weight in weights]
        gathered = [
            jnp.dot(weight.astype(jnp.bfloat16), vg[:, window], preferred_element_type=jnp.float32)
            for weight, window in zip(weights, windows)
        ]
        for window, value, total in zip(windows, gathered, totals):
            abuf[at, window] = (value / total).astype(jnp.bfloat16)

    def part_window(tile):
        return pl.ds(pl.multiple_of(tile * p_tile, p_tile), p_tile)

    def part_move(block, side, tile, far, receiver):
        slot = jnp.where(far, 1 - side, side)
        towards = jnp.where(far, block, neighbour(side))
        receiver = towards if receiver is None else receiver
        return pltpu.make_async_remote_copy(
            src_ref=pbuf.at[rows_of(block), part_window(tile)],
            dst_ref=rbuf.at[slot, rows_of(block), part_window(tile)],
            send_sem=p_send,
            recv_sem=p_recv.at[jnp.where((slot == 1) & (block == receiver), n, block), tile],
            device_id={"tensor": towards},
            device_id_type=MESH,
        )

    def part_copy(block, side, tile, far=False):
        return part_move(block, side, tile, far, None)

    def part_here(block, side, tile):
        return part_move(block, side, tile, False, me)

    def project(block, count, first_tile, send):
        at = rows_of(block, count)

        def body(index, _):
            tile = lax.rem(index + first_tile, n_out)
            window = pl.ds(pl.multiple_of(tile * o_tile, o_tile), o_tile)
            pbuf[at, window] = jnp.dot(
                abuf[at, :], wo[:, window], preferred_element_type=jnp.float32
            ).astype(jnp.bfloat16)

            @pl.when(index > 0)
            def _():
                send(lax.rem(tile + n_out - 1, n_out))

            return 0

        lax.fori_loop(0, n_out, body, 0)
        send((first_tile + n_out - 1) % n_out)

    def parts_of(tile):
        return [tile * per_out + part for part in range(per_out)]

    def drain_inputs():
        def drain_body(block, _):
            for side, sent in ((0, has_right & (block <= me)), (1, has_left & (block >= me))):
                @pl.when(sent)
                def _():
                    pltpu.make_async_remote_copy(
                        src_ref=xg.at[rows_of(block)],
                        dst_ref=xg.at[rows_of(block)],
                        send_sem=x_send.at[side, block],
                        recv_sem=x_recv.at[block, 0],
                        device_id={"tensor": neighbour(side)},
                        device_id_type=MESH,
                    ).wait_send()

            return 0

        lax.fori_loop(0, n, drain_body, 0)
        others = pl.ds(0, (frames_n - 1) * span)
        for ref, send, recv in ((kg, k_send, k_recv), (vg, v_send, v_recv)):
            pltpu.make_async_remote_copy(
                src_ref=ref.at[others],
                dst_ref=ref.at[others],
                send_sem=send,
                recv_sem=recv.at[0],
                device_id={"frame": flip(me_f, bits[0])},
                device_id_type=MESH,
            ).wait_send()

    @pl.when(jnp.logical_not(middle))
    def _():
        heading = jnp.where(has_left, -1, 1)
        arriving = jnp.where(has_left, 0, 1)
        leaving = 1 - arriving
        near = me + heading
        first = jnp.minimum(me, near)
        for chunk in range(n_x):
            q_load(chunk).wait()
            token_copy(near, arriving, chunk).wait_recv()
            q_first(first, 2, chunk)
            frame_steps(chunk)
        frames_done()
        attend(first, 2)
        for part in range(2):
            o_load(part).wait()


        def send_near(tile):
            for part in parts_of(tile):
                part_copy(near, leaving, part).start()

        project(first, 2, 0, send_near)

        def stage_body(stage, _):
            block = me + heading * stage

            def chunk_body(chunk, _):
                token_copy(block, arriving, chunk).wait_recv()
                q_step(block, 0, chunk)
                return 0

            lax.fori_loop(0, n_x, chunk_body, 0)
            attend(block, 1)

            def send_block(tile):
                for part in parts_of(tile):
                    far = jnp.logical_and(stage == n - 1, part >= chained)
                    part_copy(block, leaving, part, far).start()

            project(block, 1, 0, send_block)
            return 0

        lax.fori_loop(2, n, stage_body, 0)
        drain_inputs()

        def sum_body(tile, _):
            window = part_window(tile)
            part_here(me, arriving, tile).wait_recv()
            total = pbuf[rows_of(me), window].astype(jnp.float32)
            total = total + rbuf[arriving, rows_of(me), window].astype(jnp.float32)

            @pl.when(tile < chained)
            def _():
                out[:, window] = total.astype(jnp.bfloat16)

            @pl.when(tile >= chained)
            def _():
                part_here(me, leaving, tile).wait_recv()
                straight = rbuf[leaving, rows_of(me), window].astype(jnp.float32)
                out[:, window] = (total + straight).astype(jnp.bfloat16)

            return 0

        def sum_index(index, _):
            return sum_body(lax.rem(index + chained, n_part), 0)

        lax.fori_loop(0, n_part, sum_index, 0)

    @pl.when(middle)
    def _():
        for chunk in range(n_x):
            q_load(chunk).wait()
            for side, block in ((0, me - 1), (1, me + 1)):
                token_copy(block, side, chunk).wait_recv()
                token_copy(block, side, chunk).start()
            q_first(me - 1, 3, chunk)
            frame_steps(chunk)

        def stage_body(stage, _):
            def chunk_body(chunk, _):
                def side_body(side, _):
                    block = me - stage + 2 * side * stage

                    @pl.when(jnp.logical_and(block >= 0, block < n))
                    def _():
                        token_copy(block, side, chunk).wait_recv()
                        token_copy(block, side, chunk).start()
                        q_step(block, side, chunk)

                    return 0

                lax.fori_loop(0, 2, side_body, 0)
                return 0

            lax.fori_loop(0, n_x, chunk_body, 0)
            return 0

        lax.fori_loop(2, n - 1, stage_body, 0)
        frames_done()
        groups = max(1, n * rows // HEAD_DIM)
        while n % groups:
            groups -= 1
        count = n // groups
        for part in range(2):
            o_load(part).wait()

        def group_body(group, _):
            attend(group * count, count)

            def send_started(tile):
                last = group == groups - 1
                for part in parts_of(tile):
                    @pl.when((me == 1) & last & (part >= chained))
                    def _():
                        part_copy(n - 1, 0, part).start()

                    @pl.when((me == n - 2) & (group == 0) & (part >= chained))
                    def _():
                        part_copy(0, 1, part).start()

            project(group * count, count, chained // per_out % n_out, send_started)
            return 0

        lax.fori_loop(0, groups, group_body, 0)

        def relay(block, side, tile):
            at = rows_of(block)
            window = part_window(tile)
            part_here(block, side, tile).wait_recv()
            pbuf[at, window] = (
                pbuf[at, window].astype(jnp.float32)
                + rbuf[side, at, window].astype(jnp.float32)
            ).astype(jnp.bfloat16)
            part_copy(block, side, tile).start()

        def relay_body(index, _):
            def side_body(turn, _):
                side = jnp.where(low_half, turn, 1 - turn)
                at = index - turn * lag
                stage = 1 + lax.div(jnp.maximum(at, 0), n_part)
                tile = lax.rem(jnp.maximum(at, 0), n_part)
                block = jnp.where(side == 0, stage, n - 1 - stage)
                passes = jnp.where(side == 0, block > me, block < me)
                chain = (stage < n - 1) | ((stage == n - 1) & (tile < chained))

                @pl.when((at >= 0) & chain & passes)
                def _():
                    relay(block, side, tile)

                far = index - (n - 3) * n_part - early
                beside = jnp.where(side == 0, me == 1, me == n - 2)

                @pl.when((far >= 0) & (far < direct) & jnp.logical_not(beside))
                def _():
                    relay(jnp.where(side == 0, n - 1, 0), side, chained + far)

                return 0

            lax.fori_loop(0, 2, side_body, 0)
            return 0

        behind = jnp.minimum(me, n - 1 - me) * n_part
        lax.fori_loop(jnp.minimum(behind, (n - 3) * n_part + early), (n - 1) * n_part + lag, relay_body, 0)

        def sum_body(tile, _):
            window = part_window(tile)
            total = pbuf[rows_of(me), window].astype(jnp.float32)
            for side in range(2):
                part_here(me, side, tile).wait_recv()
                total = total + rbuf[side, rows_of(me), window].astype(jnp.float32)
            out[:, window] = total.astype(jnp.bfloat16)
            return 0

        lax.fori_loop(0, n_part, sum_body, 0)
        drain_inputs()

    others = pl.ds(0, (n - 1) * rows)
    pltpu.make_async_remote_copy(
        src_ref=pbuf.at[others],
        dst_ref=rbuf.at[0, others],
        send_sem=p_send,
        recv_sem=p_recv.at[0, 0],
        device_id={"tensor": neighbour(0)},
        device_id_type=MESH,
    ).wait_send()


def divisor(total, most):
    return math.gcd(total, most)


def per_device(
    n, frames_n,
    tokens, norm_gain, query_weight, out_weight, cache_keys, cache_values, token_pos, frame_pad
):
    rows, seqs, width = tokens.shape
    cols = query_weight.shape[1]
    span = cache_keys.shape[0]
    x_tile = divisor(width, 1024)
    o_tile = divisor(width, 512)
    p_tile = divisor(o_tile, 512)
    n_x = width // x_tile
    n_part = width // p_tile
    lag = max(1, 5 * n_part // 8)
    direct = n_part if n > 2 else 0
    early = -(3 * n_part // 8)
    hbm = pl.BlockSpec(memory_space=pltpu.HBM)
    vmem = pl.BlockSpec(memory_space=pltpu.VMEM)
    bf16 = jnp.bfloat16
    dma = pltpu.SemaphoreType.DMA
    result = pl.pallas_call(
        functools.partial(kernel, n, frames_n, x_tile, o_tile, p_tile, lag, direct, early),
        out_shape=pltpu.VMEM((rows, width), bf16),
        in_specs=[hbm, hbm, hbm, hbm, hbm, hbm, hbm, pl.BlockSpec(memory_space=pltpu.SMEM)],
        out_specs=vmem,
        scratch_shapes=[
            pltpu.VMEM(query_weight.shape, bf16),
            pltpu.VMEM(out_weight.shape, bf16),
            pltpu.VMEM((frames_n * span, cols), bf16),
            pltpu.VMEM((frames_n * span, cols), bf16),
            pltpu.VMEM((n * rows, HEAD_DIM), jnp.int32),
            pltpu.VMEM((1, width), jnp.float32),
            pltpu.VMEM((1, n * rows), jnp.int32),
            pltpu.VMEM((rows, width), bf16),
            pltpu.VMEM((n * rows, width), bf16),
            pltpu.VMEM((3 * rows, cols), jnp.float32),
            pltpu.VMEM((n * rows, cols), bf16),
            pltpu.VMEM((n * rows, cols), bf16),
            pltpu.VMEM((n * rows, width), bf16),
            pltpu.VMEM((2, n * rows, width), bf16),
            dma((n_x,)),
            dma((2,)),
            dma(()),
            dma((2,)),
            dma((2,)),
            dma(()),
            dma((frames_n // 2,)),
            dma(()),
            dma((frames_n // 2,)),
            dma((2, n)),
            dma((n, n_x)),
            dma(()),
            dma((n + 1, n_part)),
        ],
        compiler_params=pltpu.CompilerParams(collective_id=0, has_side_effects=True),
    )(
        tokens.reshape(rows, width),
        norm_gain.reshape(1, width),
        query_weight,
        out_weight,
        cache_keys.reshape(span, cols),
        cache_values.reshape(span, cols),
        token_pos.reshape(1, n * rows),
        frame_pad,
    )
    return result.reshape(rows, seqs, width)


def solution(mesh):
    placed = (
        P(("frame", "tensor"), None, None),
        P(),
        P(None, "tensor"),
        P("tensor", None),
        P("frame", None, "tensor"),
        P("frame", None, "tensor"),
        P("frame", None),
        P(),
    )
    return jax.shard_map(
        functools.partial(per_device, mesh.shape["tensor"], mesh.shape["frame"]),
        mesh=mesh,
        in_specs=placed,
        out_specs=P(("frame", "tensor"), None, None),
        check_vma=False,
    )
```

```python
import functools
import math

import jax
import jax.numpy as jnp
from jax import lax
from jax.experimental import pallas as pl
from jax.experimental.pallas import tpu as pltpu
from jax.sharding import PartitionSpec as P

HEAD_DIM = 128
epsilon = 1e-06
masked_score = -1e30
MESH = pl.DeviceIdType.MESH


def flip(index, bit):
    return index + bit - 2 * bit * lax.rem(lax.div(index, bit), 2)


def kernel(
    n, frames_n, edges, o_tile, p_tile, lag, direct, early,
    tok, gain_hbm, wq_hbm, wo_hbm, keys, values, pos_hbm, pad_hbm,
    out,
    wq, wo, kg, vg, pos_col, gain, pos, pad, raw, xg, qacc, qall, abuf, pbuf, rbuf,
    weight_sem, own_sem, small_sem, kv_own, k_send, k_recv, v_send, v_recv,
    x_send, x_recv, p_send, p_recv,
):
    me_f = lax.axis_index("frame")
    me = lax.axis_index("tensor")
    rows = tok.shape[0]
    width = tok.shape[1]
    cols = wq.shape[1]
    span = keys.shape[0]
    bits = [1 << b for b in range(int(math.log2(frames_n)))][::-1]
    phase_n = len(bits)
    k_order = bits
    v_order = bits[1::-1] + bits[2:] if phase_n > 1 else bits
    n_x = len(edges) - 1
    n_out = width // o_tile
    n_part = width // p_tile
    per_out = o_tile // p_tile
    chained = n_part - direct
    has_left = me > 0
    has_right = me < n - 1
    middle = jnp.logical_and(has_left, has_right)
    low_half = 2 * me < n

    q_load = pltpu.make_async_copy(wq_hbm, wq, weight_sem.at[0])
    o_load = pltpu.make_async_copy(wo_hbm, wo, weight_sem.at[1])

    def rows_of(block, count=1):
        return pl.ds(pl.multiple_of(block * rows, rows), count * rows)

    own_x = pltpu.make_async_copy(tok, raw, own_sem)
    own_gain = pltpu.make_async_copy(gain_hbm, gain, small_sem.at[0])
    own_pos = pltpu.make_async_copy(pos_hbm, pos, small_sem.at[1])
    own_pad = pltpu.make_async_copy(pad_hbm, pad, small_sem.at[2])
    own_k = pltpu.make_async_copy(keys, kg.at[pl.ds(0, span)], kv_own.at[0])
    own_v = pltpu.make_async_copy(values, vg.at[pl.ds(0, span)], kv_own.at[1])

    barrier = pltpu.get_barrier_semaphore()
    for bit in bits:
        pl.semaphore_signal(
            barrier, inc=1, device_id={"frame": flip(me_f, bit)}, device_id_type=MESH
        )

    @pl.when(has_left)
    def _():
        pl.semaphore_signal(barrier, inc=1, device_id={"tensor": me - 1}, device_id_type=MESH)

    @pl.when(has_right)
    def _():
        pl.semaphore_signal(barrier, inc=1, device_id={"tensor": me + 1}, device_id_type=MESH)

    own_x.start()
    own_gain.start()
    own_pos.start()
    own_pad.start()
    own_k.start()
    own_v.start()

    own_x.wait()
    own_gain.wait()
    own_k.wait()
    own_v.wait()
    q_load.start()
    o_load.start()
    hidden = raw[...].astype(jnp.float32)
    factor = lax.rsqrt(jnp.mean(hidden * hidden, axis=-1, keepdims=True) + epsilon)
    xg[rows_of(me), :] = (hidden * factor * gain[...]).astype(jnp.bfloat16)
    own_pos.wait()
    own_pad.wait()
    pos_col[...] = jnp.broadcast_to(pos[...], (HEAD_DIM, n * rows)).T

    pl.semaphore_wait(
        barrier, phase_n + has_left.astype(jnp.int32) + has_right.astype(jnp.int32)
    )

    def neighbour(side):
        return lax.rem(me + 1 - 2 * side + n, n)

    def chunk_window(chunk):
        return slice(edges[chunk], edges[chunk + 1])

    def token_copy(block, side, chunk):
        window = chunk_window(chunk)
        return pltpu.make_async_remote_copy(
            src_ref=xg.at[rows_of(block), window],
            dst_ref=xg.at[rows_of(block), window],
            send_sem=x_send,
            recv_sem=x_recv.at[block, chunk],
            device_id={"tensor": neighbour(side)},
            device_id_type=MESH,
        )

    for chunk in range(n_x):
        @pl.when(has_right)
        def _():
            token_copy(me, 0, chunk).start()

        @pl.when(has_left)
        def _():
            token_copy(me, 1, chunk).start()

    half = cols // 2

    def frame_copy(ref, slot, bit, last, piece, send, recv):
        target = slot + bit
        window = pl.ds(piece * half, half)
        index = target % last + target // (2 * last) * last
        place = recv.at[0, 0] if target & last else recv.at[piece, index]
        return pltpu.make_async_remote_copy(
            src_ref=ref.at[pl.ds(slot * span, span), window],
            dst_ref=ref.at[pl.ds(target * span, span), window],
            send_sem=send,
            recv_sem=place,
            device_id={"frame": flip(me_f, bit)},
            device_id_type=MESH,
        )

    def plan(ref, order, send, recv):
        steps, held = [], [0]
        last = order[-1]

        def copies(slot, onto):
            return [[frame_copy(ref, slot, bit, last, c, send, recv) for c in range(2)] for bit in onto]

        for p, bit in enumerate(order[:-1]):
            fresh = [slot + bit for slot in held]
            for slot in fresh:
                onward = copies(slot, order[p + 1:])
                for piece, arrival in enumerate(copies(slot - bit, [bit])[0]):
                    steps.append((arrival, [both[piece] for both in onward]))
            held = held + fresh
        own = [copy for both in copies(0, order) for copy in both]
        late = pl.ds(0, len(held) * span)
        rest = pltpu.make_async_remote_copy(
            src_ref=ref.at[late],
            dst_ref=ref.at[late],
            send_sem=send,
            recv_sem=recv.at[0, 0],
            device_id={"frame": flip(me_f, last)},
            device_id_type=MESH,
        )
        return own, steps, rest

    k_own, k_steps, k_rest = plan(kg, k_order, k_send, k_recv)
    v_own, v_steps, v_rest = plan(vg, v_order, v_send, v_recv)
    for pair in zip(k_own, v_own):
        for copy in pair:
            copy.start()
    relays = list(zip(k_steps, v_steps))
    cuts = [0] + [len(relays) * (i + 1) // (n_x + 2) for i in range(n_x)] + [len(relays)]

    def frame_steps(turn):
        for pair in relays[cuts[turn]:cuts[turn + 1]]:
            for arrival, onward in pair:
                arrival.wait_recv()
                for copy in onward:
                    copy.start()

    def frames_done():
        k_rest.wait_recv()
        v_rest.wait_recv()

    slot_of = lax.broadcasted_iota(jnp.int32, (1, span), 1)
    pieces = []
    for slot in range(frames_n):
        owner = me_f
        for bit in bits:
            if slot & bit:
                owner = flip(owner, bit)
        pieces.append(slot_of + owner * span)
    frame_index = jnp.concatenate(pieces, axis=1)
    visible_frames = frame_index < frames_n * span - pad[...]

    scale = HEAD_DIM ** (-0.5)

    def q_step(block, count, place, chunk):
        window = chunk_window(chunk)
        at = rows_of(block, count)
        held = rows_of(place, count)
        product = jnp.dot(xg[at, window], wq[window, :], preferred_element_type=jnp.float32)
        if chunk > 0:
            product = qacc[held, :] + product
        if chunk < n_x - 1:
            qacc[held, :] = product
        else:
            qall[at, :] = (product * scale).astype(jnp.bfloat16)

    def attend(block, count):
        at = rows_of(block, count)
        visible = (frame_index <= pos_col[at, :1]) & visible_frames
        windows = [slice(i, i + HEAD_DIM) for i in range(0, cols, HEAD_DIM)]
        scores = [
            lax.dot_general(
                qall[at, window], kg[:, window], (((1,), (1,)), ((), ())),
                preferred_element_type=jnp.float32,
            )
            for window in windows
        ]
        scores = [jnp.where(visible, score, masked_score) for score in scores]
        highest = [jnp.max(score, axis=-1, keepdims=True) for score in scores]
        weights = [
            jnp.where(visible, jnp.exp(score - top), 0.0) for score, top in zip(scores, highest)
        ]
        totals = [jnp.sum(weight, axis=-1, keepdims=True) for weight in weights]
        gathered = [
            jnp.dot(weight.astype(jnp.bfloat16), vg[:, window], preferred_element_type=jnp.float32)
            for weight, window in zip(weights, windows)
        ]
        for window, value, total in zip(windows, gathered, totals):
            abuf[at, window] = (value / total).astype(jnp.bfloat16)

    def part_window(tile):
        return pl.ds(pl.multiple_of(tile * p_tile, p_tile), p_tile)

    def part_move(block, side, tile, far, receiver):
        slot = jnp.where(far, 1 - side, side)
        towards = jnp.where(far, block, neighbour(side))
        receiver = towards if receiver is None else receiver
        return pltpu.make_async_remote_copy(
            src_ref=pbuf.at[rows_of(block), part_window(tile)],
            dst_ref=rbuf.at[slot, rows_of(block), part_window(tile)],
            send_sem=p_send,
            recv_sem=p_recv.at[jnp.where((slot == 1) & (block == receiver), n, block), tile],
            device_id={"tensor": towards},
            device_id_type=MESH,
        )

    def part_copy(block, side, tile, far=False):
        return part_move(block, side, tile, far, None)

    def part_here(block, side, tile):
        return part_move(block, side, tile, False, me)

    def project(block, count, first_tile, send):
        at = rows_of(block, count)

        def body(index, _):
            tile = lax.rem(index + first_tile, n_out)
            window = pl.ds(pl.multiple_of(tile * o_tile, o_tile), o_tile)
            pbuf[at, window] = jnp.dot(
                abuf[at, :], wo[:, window], preferred_element_type=jnp.float32
            ).astype(jnp.bfloat16)

            if send is not None:
                send(tile)
            return 0

        lax.fori_loop(0, n_out, body, 0)

    def parts_of(tile):
        return [tile * per_out + part for part in range(per_out)]

    def drain_inputs():
        def drain_tokens(count):
            sent = pl.ds(0, count * rows)
            pltpu.make_async_remote_copy(
                src_ref=xg.at[sent],
                dst_ref=xg.at[sent],
                send_sem=x_send,
                recv_sem=x_recv.at[0, 0],
                device_id={"tensor": neighbour(0)},
                device_id_type=MESH,
            ).wait_send()

        @pl.when(middle)
        def _():
            drain_tokens(n + 1)

        @pl.when(jnp.logical_not(middle))
        def _():
            drain_tokens(1)

        others = pl.ds(0, (frames_n - 1) * span)
        for ref, send, recv in ((kg, k_send, k_recv), (vg, v_send, v_recv)):
            pltpu.make_async_remote_copy(
                src_ref=ref.at[others],
                dst_ref=ref.at[others],
                send_sem=send,
                recv_sem=recv.at[0, 0],
                device_id={"frame": flip(me_f, bits[0])},
                device_id_type=MESH,
            ).wait_send()

    @pl.when(jnp.logical_not(middle))
    def _():
        heading = jnp.where(has_left, -1, 1)
        arriving = jnp.where(has_left, 0, 1)
        leaving = 1 - arriving
        near = me + heading
        first = jnp.minimum(me, near)
        frame_steps(0)
        q_load.wait()
        for chunk in range(n_x):
            token_copy(near, arriving, chunk).wait_recv()
            q_step(first, 2, 0, chunk)
            frame_steps(chunk + 1)
        frames_done()
        attend(near, 1)
        o_load.wait()


        def send_near(tile):
            for part in parts_of(tile):
                part_copy(near, leaving, part).start()

        project(near, 1, 0, send_near)

        def stage_body(stage, _):
            block = me + heading * stage

            for chunk in range(n_x):
                token_copy(block, arriving, chunk).wait_recv()
                q_step(block, 1, 0, chunk)
            attend(block, 1)

            def send_block(tile):
                for part in parts_of(tile):
                    far = jnp.logical_and(stage == n - 1, part >= chained)
                    part_copy(block, leaving, part, far).start()

            project(block, 1, 0, send_block)
            return 0

        lax.fori_loop(2, n, stage_body, 0)
        attend(me, 1)
        project(me, 1, 0, None)
        drain_inputs()

        def sum_body(tile, _):
            window = part_window(tile)
            part_here(me, arriving, tile).wait_recv()
            total = pbuf[rows_of(me), window].astype(jnp.float32)
            total = total + rbuf[arriving, rows_of(me), window].astype(jnp.float32)

            @pl.when(tile < chained)
            def _():
                out[:, window] = total.astype(jnp.bfloat16)

            @pl.when(tile >= chained)
            def _():
                part_here(me, leaving, tile).wait_recv()
                straight = rbuf[leaving, rows_of(me), window].astype(jnp.float32)
                out[:, window] = (total + straight).astype(jnp.bfloat16)

            return 0

        def sum_index(index, _):
            return sum_body(lax.rem(index + chained, n_part), 0)

        lax.fori_loop(0, n_part, sum_index, 0)

    @pl.when(middle)
    def _():
        frame_steps(0)
        q_load.wait()
        for chunk in range(n_x):
            for side, block in ((0, me - 1), (1, me + 1)):
                token_copy(block, side, chunk).wait_recv()
                token_copy(block, side, chunk).start()
            q_step(me - 1, 3, 0, chunk)
            frame_steps(chunk + 1)

        def near_attend():
            frames_done()
            attend(me - 1, 3)

        def stage_body(stage, _):
            for chunk in range(n_x):
                def side_body(side, _):
                    block = me - stage + 2 * side * stage

                    @pl.when(jnp.logical_and(block >= 0, block < n))
                    def _():
                        token_copy(block, side, chunk).wait_recv()
                        token_copy(block, side, chunk).start()
                        q_step(block, 1, side, chunk)

                    return 0

                lax.fori_loop(0, 2, side_body, 0)
                if chunk == 0:
                    pl.when(stage == 2)(near_attend)

            def attend_body(side, _):
                block = me - stage + 2 * side * stage

                @pl.when(jnp.logical_and(block >= 0, block < n))
                def _():
                    attend(block, 1)

                return 0

            lax.fori_loop(0, 2, attend_body, 0)
            return 0

        if n == 3:
            near_attend()
        lax.fori_loop(2, n - 1, stage_body, 0)
        groups = max(1, n * rows // HEAD_DIM)
        while n % groups:
            groups -= 1
        count = n // groups
        o_load.wait()

        def group_body(group, _):
            def send_started(tile):
                last = group == groups - 1
                for part in parts_of(tile):
                    @pl.when((me == 1) & last & (part >= chained))
                    def _():
                        part_copy(n - 1, 0, part).start()

                    @pl.when((me == n - 2) & (group == 0) & (part >= chained))
                    def _():
                        part_copy(0, 1, part).start()

            project(group * count, count, chained // per_out % n_out, send_started)
            return 0

        lax.fori_loop(0, groups, group_body, 0)

        def relay(block, side, tile):
            at = rows_of(block)
            window = part_window(tile)
            part_here(block, side, tile).wait_recv()
            pbuf[at, window] = (
                pbuf[at, window].astype(jnp.float32)
                + rbuf[side, at, window].astype(jnp.float32)
            ).astype(jnp.bfloat16)
            part_copy(block, side, tile).start()

        def relay_body(index, _):
            def side_body(turn, _):
                side = jnp.where(low_half, turn, 1 - turn)
                at = index - turn * lag
                stage = 1 + lax.div(jnp.maximum(at, 0), n_part)
                tile = lax.rem(jnp.maximum(at, 0), n_part)
                block = jnp.where(side == 0, stage, n - 1 - stage)
                passes = jnp.where(side == 0, block > me, block < me)
                chain = (stage < n - 1) | ((stage == n - 1) & (tile < chained))

                @pl.when((at >= 0) & chain & passes)
                def _():
                    relay(block, side, tile)

                far = index - (n - 3) * n_part - early
                beside = jnp.where(side == 0, me == 1, me == n - 2)

                @pl.when((far >= 0) & (far < direct) & jnp.logical_not(beside))
                def _():
                    relay(jnp.where(side == 0, n - 1, 0), side, chained + far)

                return 0

            lax.fori_loop(0, 2, side_body, 0)
            return 0

        behind = jnp.minimum(me, n - 1 - me) * n_part
        lax.fori_loop(jnp.minimum(behind, (n - 3) * n_part + early), (n - 1) * n_part + lag, relay_body, 0)

        def sum_body(tile, _):
            window = part_window(tile)
            total = pbuf[rows_of(me), window].astype(jnp.float32)
            for side in range(2):
                part_here(me, side, tile).wait_recv()
                total = total + rbuf[side, rows_of(me), window].astype(jnp.float32)
            out[:, window] = total.astype(jnp.bfloat16)
            return 0

        lax.fori_loop(0, n_part, sum_body, 0)
        drain_inputs()

    others = pl.ds(0, (n - 1) * rows)
    pltpu.make_async_remote_copy(
        src_ref=pbuf.at[others],
        dst_ref=rbuf.at[0, others],
        send_sem=p_send,
        recv_sem=p_recv.at[0, 0],
        device_id={"tensor": neighbour(0)},
        device_id_type=MESH,
    ).wait_send()


def divisor(total, most):
    return math.gcd(total, most)


def per_device(
    n, frames_n,
    tokens, norm_gain, query_weight, out_weight, cache_keys, cache_values, token_pos, frame_pad
):
    rows, seqs, width = tokens.shape
    cols = query_weight.shape[1]
    span = cache_keys.shape[0]
    unit = divisor(width, 256)
    shares = (6, 5, 3, 2)
    edges = [width // unit * sum(shares[:i]) // sum(shares) * unit for i in range(len(shares) + 1)]
    o_tile = divisor(width, 512)
    p_tile = divisor(o_tile, 512)
    n_x = len(shares)
    n_part = width // p_tile
    lag = max(1, 5 * n_part // 8)
    direct = n_part if n > 2 else 0
    early = -(3 * n_part // 8)
    hbm = pl.BlockSpec(memory_space=pltpu.HBM)
    vmem = pl.BlockSpec(memory_space=pltpu.VMEM)
    bf16 = jnp.bfloat16
    dma = pltpu.SemaphoreType.DMA
    result = pl.pallas_call(
        functools.partial(kernel, n, frames_n, edges, o_tile, p_tile, lag, direct, early),
        out_shape=pltpu.VMEM((rows, width), bf16),
        in_specs=[hbm] * 8,
        out_specs=vmem,
        scratch_shapes=[
            pltpu.VMEM(query_weight.shape, bf16),
            pltpu.VMEM(out_weight.shape, bf16),
            pltpu.VMEM((frames_n * span, cols), bf16),
            pltpu.VMEM((frames_n * span, cols), bf16),
            pltpu.VMEM((n * rows, HEAD_DIM), jnp.int32),
            pltpu.VMEM((1, width), jnp.float32),
            pltpu.VMEM((1, n * rows), jnp.int32),
            pltpu.VMEM((1, 1), jnp.int32),
            pltpu.VMEM((rows, width), bf16),
            pltpu.VMEM(((n + 1) * rows, width), bf16),
            pltpu.VMEM((3 * rows, cols), jnp.float32),
            pltpu.VMEM((n * rows, cols), bf16),
            pltpu.VMEM((n * rows, cols), bf16),
            pltpu.VMEM((n * rows, width), bf16),
            pltpu.VMEM((2, n * rows, width), bf16),
            dma((2,)),
            dma(()),
            dma((3,)),
            dma((2,)),
            dma(()),
            dma((2, frames_n // 2)),
            dma(()),
            dma((2, frames_n // 2)),
            dma(()),
            dma((n, n_x)),
            dma(()),
            dma((n + 1, n_part)),
        ],
        compiler_params=pltpu.CompilerParams(collective_id=0, has_side_effects=True),
    )(
        tokens.reshape(rows, width),
        norm_gain.reshape(1, width),
        query_weight,
        out_weight,
        cache_keys.reshape(span, cols),
        cache_values.reshape(span, cols),
        token_pos.reshape(1, n * rows),
        frame_pad.reshape(1, 1),
    )
    return result.reshape(rows, seqs, width)


def solution(mesh):
    placed = (
        P(("frame", "tensor"), None, None),
        P(),
        P(None, "tensor"),
        P("tensor", None),
        P("frame", None, "tensor"),
        P("frame", None, "tensor"),
        P("frame", None),
        P(),
    )
    return jax.shard_map(
        functools.partial(per_device, mesh.shape["tensor"], mesh.shape["frame"]),
        mesh=mesh,
        in_specs=placed,
        out_specs=P(("frame", "tensor"), None, None),
        check_vma=False,
    )
```

```python
import functools
import math

import jax
import jax.numpy as jnp
from jax import lax
from jax.experimental import pallas as pl
from jax.experimental.pallas import tpu as pltpu
from jax.sharding import PartitionSpec as P

HEAD_DIM = 128
epsilon = 1e-06
masked_score = -1e30
MESH = pl.DeviceIdType.MESH


def flip(index, bit):
    return index + bit - 2 * bit * lax.rem(lax.div(index, bit), 2)


def kernel(
    n, frames_n, edges, o_tile, p_tile, lag, direct, early, carry, defer,
    tok, gain_hbm, wq_hbm, wo_hbm, keys, values, pos_hbm, pad_hbm,
    out,
    wq, wo, kg, vg, pos_col, gain, pos, pad, raw, xg, qacc, qall, abuf, pbuf, rbuf,
    weight_sem, own_sem, small_sem, kv_own, k_send, k_recv, v_send, v_recv,
    x_send, x_recv, p_send, p_recv,
):
    me_f = lax.axis_index("frame")
    me = lax.axis_index("tensor")
    rows = tok.shape[0]
    width = tok.shape[1]
    cols = wq.shape[1]
    span = keys.shape[0]
    bits = [1 << b for b in range(int(math.log2(frames_n)))][::-1]
    phase_n = len(bits)
    k_order = bits
    v_order = bits[1::-1] + bits[2:] if phase_n > 1 else bits
    n_x = len(edges) - 1
    n_out = width // o_tile
    n_part = width // p_tile
    per_out = o_tile // p_tile
    chained = n_part - direct
    alone = n_part - carry
    has_left = me > 0
    has_right = me < n - 1
    middle = jnp.logical_and(has_left, has_right)
    low_half = 2 * me < n

    q_load = pltpu.make_async_copy(wq_hbm, wq, weight_sem.at[0])
    o_load = pltpu.make_async_copy(wo_hbm, wo, weight_sem.at[1])

    def rows_of(block, count=1):
        return pl.ds(pl.multiple_of(block * rows, rows), count * rows)

    own_x = pltpu.make_async_copy(tok, raw, own_sem)
    own_gain = pltpu.make_async_copy(gain_hbm, gain, small_sem.at[0])
    own_pos = pltpu.make_async_copy(pos_hbm, pos, small_sem.at[1])
    own_pad = pltpu.make_async_copy(pad_hbm, pad, small_sem.at[2])
    own_k = pltpu.make_async_copy(keys, kg.at[pl.ds(0, span)], kv_own.at[0])
    own_v = pltpu.make_async_copy(values, vg.at[pl.ds(0, span)], kv_own.at[1])

    barrier = pltpu.get_barrier_semaphore()
    for bit in bits:
        pl.semaphore_signal(
            barrier, inc=1, device_id={"frame": flip(me_f, bit)}, device_id_type=MESH
        )

    @pl.when(has_left)
    def _():
        pl.semaphore_signal(barrier, inc=1, device_id={"tensor": me - 1}, device_id_type=MESH)

    @pl.when(has_right)
    def _():
        pl.semaphore_signal(barrier, inc=1, device_id={"tensor": me + 1}, device_id_type=MESH)

    own_x.start()
    own_gain.start()
    own_pos.start()
    own_pad.start()
    own_k.start()
    own_v.start()

    own_x.wait()
    own_gain.wait()
    own_k.wait()
    own_v.wait()
    q_load.start()
    o_load.start()
    hidden = raw[...].astype(jnp.float32)
    factor = lax.rsqrt(jnp.mean(hidden * hidden, axis=-1, keepdims=True) + epsilon)
    xg[rows_of(me), :] = (hidden * factor * gain[...]).astype(jnp.bfloat16)
    own_pos.wait()
    own_pad.wait()
    pos_col[...] = jnp.broadcast_to(pos[...], (HEAD_DIM, n * rows)).T

    pl.semaphore_wait(
        barrier, phase_n + has_left.astype(jnp.int32) + has_right.astype(jnp.int32)
    )

    def neighbour(side):
        return lax.rem(me + 1 - 2 * side + n, n)

    def chunk_window(chunk):
        return slice(edges[chunk], edges[chunk + 1])

    def token_copy(block, side, chunk):
        window = chunk_window(chunk)
        return pltpu.make_async_remote_copy(
            src_ref=xg.at[rows_of(block), window],
            dst_ref=xg.at[rows_of(block), window],
            send_sem=x_send,
            recv_sem=x_recv.at[block, chunk],
            device_id={"tensor": neighbour(side)},
            device_id_type=MESH,
        )

    for chunk in range(n_x):
        @pl.when(has_right)
        def _():
            token_copy(me, 0, chunk).start()

        @pl.when(has_left)
        def _():
            token_copy(me, 1, chunk).start()

    half = cols // 2

    def frame_copy(ref, slot, bit, last, piece, send, recv):
        target = slot + bit
        window = pl.ds(piece * half, half)
        index = target % last + target // (2 * last) * last
        place = recv.at[0, 0] if target & last else recv.at[piece, index]
        return pltpu.make_async_remote_copy(
            src_ref=ref.at[pl.ds(slot * span, span), window],
            dst_ref=ref.at[pl.ds(target * span, span), window],
            send_sem=send,
            recv_sem=place,
            device_id={"frame": flip(me_f, bit)},
            device_id_type=MESH,
        )

    def plan(ref, order, send, recv):
        steps, held = [], [0]
        last = order[-1]

        def copies(slot, onto):
            return [[frame_copy(ref, slot, bit, last, c, send, recv) for c in range(2)] for bit in onto]

        for p, bit in enumerate(order[:-1]):
            fresh = [slot + bit for slot in held]
            for slot in fresh:
                onward = copies(slot, order[p + 1:])
                for piece, arrival in enumerate(copies(slot - bit, [bit])[0]):
                    steps.append((arrival, [both[piece] for both in onward]))
            held = held + fresh
        own = [copy for both in copies(0, order) for copy in both]
        late = pl.ds(0, len(held) * span)
        rest = pltpu.make_async_remote_copy(
            src_ref=ref.at[late],
            dst_ref=ref.at[late],
            send_sem=send,
            recv_sem=recv.at[0, 0],
            device_id={"frame": flip(me_f, last)},
            device_id_type=MESH,
        )
        return own, steps, rest

    k_own, k_steps, k_rest = plan(kg, k_order, k_send, k_recv)
    v_own, v_steps, v_rest = plan(vg, v_order, v_send, v_recv)
    for pair in zip(k_own, v_own):
        for copy in pair:
            copy.start()
    relays = list(zip(k_steps, v_steps))
    cuts = [0] + [len(relays) * (i + 1) // (n_x + 2) for i in range(n_x)] + [len(relays)]

    def frame_steps(turn):
        for pair in relays[cuts[turn]:cuts[turn + 1]]:
            for arrival, onward in pair:
                arrival.wait_recv()
                for copy in onward:
                    copy.start()

    def frames_done():
        k_rest.wait_recv()
        v_rest.wait_recv()

    slot_of = lax.broadcasted_iota(jnp.int32, (1, span), 1)
    pieces = []
    for slot in range(frames_n):
        owner = me_f
        for bit in bits:
            if slot & bit:
                owner = flip(owner, bit)
        pieces.append(slot_of + owner * span)
    frame_index = jnp.concatenate(pieces, axis=1)
    visible_frames = frame_index < frames_n * span - pad[...]

    scale = HEAD_DIM ** (-0.5)

    def q_step(block, count, place, chunk):
        window = chunk_window(chunk)
        at = rows_of(block, count)
        held = rows_of(place, count)
        product = jnp.dot(xg[at, window], wq[window, :], preferred_element_type=jnp.float32)
        if chunk > 0:
            product = qacc[held, :] + product
        if chunk < n_x - 1:
            qacc[held, :] = product
        else:
            qall[at, :] = (product * scale).astype(jnp.bfloat16)

    def attend(block, count):
        at = rows_of(block, count)
        visible = (frame_index <= pos_col[at, :1]) & visible_frames
        windows = [slice(i, i + HEAD_DIM) for i in range(0, cols, HEAD_DIM)]
        scores = [
            lax.dot_general(
                qall[at, window], kg[:, window], (((1,), (1,)), ((), ())),
                preferred_element_type=jnp.float32,
            )
            for window in windows
        ]
        scores = [jnp.where(visible, score, masked_score) for score in scores]
        highest = [jnp.max(score, axis=-1, keepdims=True) for score in scores]
        weights = [jnp.exp(score - top) for score, top in zip(scores, highest)]
        totals = [jnp.sum(weight, axis=-1, keepdims=True) for weight in weights]
        gathered = [
            jnp.dot(weight.astype(jnp.bfloat16), vg[:, window], preferred_element_type=jnp.float32)
            for weight, window in zip(weights, windows)
        ]
        for window, value, total in zip(windows, gathered, totals):
            abuf[at, window] = (value / total).astype(jnp.bfloat16)

    def part_window(tile):
        return pl.ds(pl.multiple_of(tile * p_tile, p_tile), p_tile)

    def part_move(block, side, tile, far, receiver):
        slot = jnp.where(far, 1 - side, side)
        towards = jnp.where(far, block, neighbour(side))
        receiver = towards if receiver is None else receiver
        return pltpu.make_async_remote_copy(
            src_ref=pbuf.at[rows_of(block), part_window(tile)],
            dst_ref=rbuf.at[slot, rows_of(block), part_window(tile)],
            send_sem=p_send,
            recv_sem=p_recv.at[jnp.where((slot == 1) & (block == receiver), n, block), tile],
            device_id={"tensor": towards},
            device_id_type=MESH,
        )

    def part_copy(block, side, tile, far=False):
        return part_move(block, side, tile, far, None)

    def part_here(block, side, tile):
        return part_move(block, side, tile, False, me)

    def project(block, count, first_tile, send):
        at = rows_of(block, count)

        def body(index, _):
            tile = lax.rem(index + first_tile, n_out)
            window = pl.ds(pl.multiple_of(tile * o_tile, o_tile), o_tile)
            pbuf[at, window] = jnp.dot(
                abuf[at, :], wo[:, window], preferred_element_type=jnp.float32
            ).astype(jnp.bfloat16)

            if send is not None:
                send(tile)
            return 0

        lax.fori_loop(0, n_out, body, 0)

    def add_part(block, side, tile):
        at = rows_of(block)
        window = part_window(tile)
        part_here(block, side, tile).wait_recv()
        pbuf[at, window] = (
            pbuf[at, window].astype(jnp.float32) + rbuf[side, at, window].astype(jnp.float32)
        ).astype(jnp.bfloat16)

    def parts_of(tile):
        return [tile * per_out + part for part in range(per_out)]

    def drain_inputs():
        def drain_tokens(count):
            sent = pl.ds(0, count * rows)
            pltpu.make_async_remote_copy(
                src_ref=xg.at[sent],
                dst_ref=xg.at[sent],
                send_sem=x_send,
                recv_sem=x_recv.at[0, 0],
                device_id={"tensor": neighbour(0)},
                device_id_type=MESH,
            ).wait_send()

        @pl.when(middle)
        def _():
            drain_tokens(n + 1)

        @pl.when(jnp.logical_not(middle))
        def _():
            drain_tokens(1)

        others = pl.ds(0, (frames_n - 1) * span)
        for ref, send, recv in ((kg, k_send, k_recv), (vg, v_send, v_recv)):
            pltpu.make_async_remote_copy(
                src_ref=ref.at[others],
                dst_ref=ref.at[others],
                send_sem=send,
                recv_sem=recv.at[0, 0],
                device_id={"frame": flip(me_f, bits[0])},
                device_id_type=MESH,
            ).wait_send()

    @pl.when(jnp.logical_not(middle))
    def _():
        heading = jnp.where(has_left, -1, 1)
        arriving = jnp.where(has_left, 0, 1)
        leaving = 1 - arriving
        near = me + heading
        first = jnp.minimum(me, near)
        frame_steps(0)
        q_load.wait()
        for chunk in range(n_x):
            token_copy(near, arriving, chunk).wait_recv()
            q_step(first, 2, 0, chunk)
            frame_steps(chunk + 1)
        frames_done()
        attend(near, 1)
        o_load.wait()

        def send_near(tile):
            for part in parts_of(tile):
                @pl.when(part < n_part - defer)
                def _():
                    part_copy(near, leaving, part).start()

        project(near, 1, 0, send_near)

        def stage_body(stage, _):
            block = me + heading * stage

            for chunk in range(n_x):
                token_copy(block, arriving, chunk).wait_recv()
                q_step(block, 1, 0, chunk)
            attend(block, 1)

            def send_block(tile):
                for part in parts_of(tile):
                    far = jnp.logical_and(stage == n - 1, part >= chained)

                    @pl.when(far & has_left & (part >= alone))
                    def _():
                        add_part(block, 0, part)

                    part_copy(block, leaving, part, far).start()

            project(block, 1, 0, send_block)
            return 0

        lax.fori_loop(2, n, stage_body, 0)
        for part in range(n_part - defer, n_part):
            part_copy(near, leaving, part).start()
        attend(me, 1)
        project(me, 1, 0, None)
        drain_inputs()

        def sum_body(tile, _):
            window = part_window(tile)
            part_here(me, arriving, tile).wait_recv()
            total = pbuf[rows_of(me), window].astype(jnp.float32)
            total = total + rbuf[arriving, rows_of(me), window].astype(jnp.float32)

            @pl.when(tile < chained)
            def _():
                out[:, window] = total.astype(jnp.bfloat16)

            @pl.when(tile >= chained)
            def _():
                part_here(me, leaving, tile).wait_recv()
                straight = rbuf[leaving, rows_of(me), window].astype(jnp.float32)
                out[:, window] = (total + straight).astype(jnp.bfloat16)

            return 0

        def sum_index(index, _):
            return sum_body(lax.rem(index + chained, n_part), 0)

        lax.fori_loop(0, n_part, sum_index, 0)

    @pl.when(middle)
    def _():
        frame_steps(0)
        q_load.wait()
        for chunk in range(n_x):
            for side, block in ((0, me - 1), (1, me + 1)):
                token_copy(block, side, chunk).wait_recv()
                token_copy(block, side, chunk).start()
            q_step(me - 1, 3, 0, chunk)
            frame_steps(chunk + 1)

        def near_attend():
            frames_done()
            attend(me - 1, 3)

        def stage_body(stage, _):
            for chunk in range(n_x):
                def side_body(side, _):
                    block = me - stage + 2 * side * stage

                    @pl.when(jnp.logical_and(block >= 0, block < n))
                    def _():
                        token_copy(block, side, chunk).wait_recv()
                        token_copy(block, side, chunk).start()
                        q_step(block, 1, side, chunk)

                    return 0

                lax.fori_loop(0, 2, side_body, 0)
                if chunk == 0:
                    pl.when(stage == 2)(near_attend)

            def attend_body(side, _):
                block = me - stage + 2 * side * stage

                @pl.when(jnp.logical_and(block >= 0, block < n))
                def _():
                    attend(block, 1)

                return 0

            lax.fori_loop(0, 2, attend_body, 0)
            return 0

        if n == 3:
            near_attend()
        lax.fori_loop(2, n - 1, stage_body, 0)
        groups = max(1, n * rows // HEAD_DIM)
        while n % groups:
            groups -= 1
        count = n // groups
        o_load.wait()

        def group_body(group, _):
            def send_started(tile):
                last = group == groups - 1
                for part in parts_of(tile):
                    @pl.when((me == 1) & last & (part >= chained))
                    def _():
                        part_copy(n - 1, 0, part).start()

                    carried = part >= alone
                    begins = jnp.where(carried, me == n - 3, me == n - 2)

                    @pl.when(begins & (group == 0) & (part >= chained))
                    def _():
                        part_copy(0, 1, part).start()

            project(group * count, count, chained // per_out % n_out, send_started)
            return 0

        lax.fori_loop(0, groups, group_body, 0)

        @pl.when(me == n - 2)
        def _():
            for part in range(alone, n_part):
                part_copy(0, 0, part).start()

        def relay(block, side, tile):
            add_part(block, side, tile)
            part_copy(block, side, tile).start()

        def relay_body(index, _):
            def side_body(turn, _):
                side = jnp.where(low_half, turn, 1 - turn)
                at = index - turn * lag
                stage = 1 + lax.div(jnp.maximum(at, 0), n_part)
                tile = lax.rem(jnp.maximum(at, 0), n_part)
                block = jnp.where(side == 0, stage, n - 1 - stage)
                passes = jnp.where(side == 0, block > me, block < me)
                chain = (stage < n - 1) | ((stage == n - 1) & (tile < chained))

                @pl.when((at >= 0) & chain & passes)
                def _():
                    relay(block, side, tile)

                far = index - (n - 3) * n_part - early
                carried = chained + far >= alone
                beside = jnp.where(side == 0, me == 1, (me == n - 2) | (carried & (me == n - 3)))

                @pl.when((far >= 0) & (far < direct) & jnp.logical_not(beside))
                def _():
                    relay(jnp.where(side == 0, n - 1, 0), side, chained + far)

                return 0

            lax.fori_loop(0, 2, side_body, 0)
            return 0

        behind = jnp.minimum(me, n - 1 - me) * n_part
        lax.fori_loop(jnp.minimum(behind, (n - 3) * n_part + early), (n - 1) * n_part + lag, relay_body, 0)

        def sum_body(tile, _):
            window = part_window(tile)
            total = pbuf[rows_of(me), window].astype(jnp.float32)
            for side in range(2):
                part_here(me, side, tile).wait_recv()
                total = total + rbuf[side, rows_of(me), window].astype(jnp.float32)
            out[:, window] = total.astype(jnp.bfloat16)
            return 0

        lax.fori_loop(0, n_part, sum_body, 0)
        drain_inputs()

    others = pl.ds(0, (n - 1) * rows)
    pltpu.make_async_remote_copy(
        src_ref=pbuf.at[others],
        dst_ref=rbuf.at[0, others],
        send_sem=p_send,
        recv_sem=p_recv.at[0, 0],
        device_id={"tensor": neighbour(0)},
        device_id_type=MESH,
    ).wait_send()


def divisor(total, most):
    return math.gcd(total, most)


def per_device(
    n, frames_n,
    tokens, norm_gain, query_weight, out_weight, cache_keys, cache_values, token_pos, frame_pad
):
    rows, seqs, width = tokens.shape
    cols = query_weight.shape[1]
    span = cache_keys.shape[0]
    unit = divisor(width, 256)
    shares = (6, 5, 3, 2)
    edges = [width // unit * sum(shares[:i]) // sum(shares) * unit for i in range(len(shares) + 1)]
    o_tile = divisor(width, 512)
    p_tile = divisor(o_tile, 512)
    n_x = len(shares)
    n_part = width // p_tile
    lag = max(1, 5 * n_part // 8)
    direct = n_part if n > 2 else 0
    early = -(3 * n_part // 8)
    carry = 3 * n_part // 8 if n > 3 else 0
    defer = n_part // 8 if n > 3 else 0
    hbm = pl.BlockSpec(memory_space=pltpu.HBM)
    vmem = pl.BlockSpec(memory_space=pltpu.VMEM)
    bf16 = jnp.bfloat16
    dma = pltpu.SemaphoreType.DMA
    result = pl.pallas_call(
        functools.partial(kernel, n, frames_n, edges, o_tile, p_tile, lag, direct, early, carry, defer),
        out_shape=pltpu.VMEM((rows, width), bf16),
        in_specs=[hbm] * 8,
        out_specs=vmem,
        scratch_shapes=[
            pltpu.VMEM(query_weight.shape, bf16),
            pltpu.VMEM(out_weight.shape, bf16),
            pltpu.VMEM((frames_n * span, cols), bf16),
            pltpu.VMEM((frames_n * span, cols), bf16),
            pltpu.VMEM((n * rows, HEAD_DIM), jnp.int32),
            pltpu.VMEM((1, width), jnp.float32),
            pltpu.VMEM((1, n * rows), jnp.int32),
            pltpu.VMEM((1, 1), jnp.int32),
            pltpu.VMEM((rows, width), bf16),
            pltpu.VMEM(((n + 1) * rows, width), bf16),
            pltpu.VMEM((3 * rows, cols), jnp.float32),
            pltpu.VMEM((n * rows, cols), bf16),
            pltpu.VMEM((n * rows, cols), bf16),
            pltpu.VMEM((n * rows, width), bf16),
            pltpu.VMEM((2, n * rows, width), bf16),
            dma((2,)),
            dma(()),
            dma((3,)),
            dma((2,)),
            dma(()),
            dma((2, frames_n // 2)),
            dma(()),
            dma((2, frames_n // 2)),
            dma(()),
            dma((n, n_x)),
            dma(()),
            dma((n + 1, n_part)),
        ],
        compiler_params=pltpu.CompilerParams(collective_id=0, has_side_effects=True),
    )(
        tokens.reshape(rows, width),
        norm_gain.reshape(1, width),
        query_weight,
        out_weight,
        cache_keys.reshape(span, cols),
        cache_values.reshape(span, cols),
        token_pos.reshape(1, n * rows),
        frame_pad.reshape(1, 1),
    )
    return result.reshape(rows, seqs, width)


def solution(mesh):
    placed = (
        P(("frame", "tensor"), None, None),
        P(),
        P(None, "tensor"),
        P("tensor", None),
        P("frame", None, "tensor"),
        P("frame", None, "tensor"),
        P("frame", None),
        P(),
    )
    return jax.shard_map(
        functools.partial(per_device, mesh.shape["tensor"], mesh.shape["frame"]),
        mesh=mesh,
        in_specs=placed,
        out_specs=P(("frame", "tensor"), None, None),
        check_vma=False,
    )
```

```python
import functools
import math

import jax
import jax.numpy as jnp
from jax import lax
from jax.experimental import pallas as pl
from jax.experimental.pallas import tpu as pltpu
from jax.sharding import PartitionSpec as P

HEAD_DIM = 128
epsilon = 1e-06
masked_score = -1e30
MESH = pl.DeviceIdType.MESH


def flip(index, bit):
    return index + bit - 2 * bit * lax.rem(lax.div(index, bit), 2)


def kernel(
    n, frames_n, edges, o_tile, p_tile, lag, direct, early, carry, defer,
    tok, gain_hbm, wq_hbm, wo_hbm, keys, values, pos_hbm, pad_hbm,
    out,
    wq, wo, kg, vg, pos_col, gain, pos, pad, raw, xg, qacc, qall, abuf, pbuf, rbuf,
    weight_sem, own_sem, small_sem, kv_own, k_send, k_recv, v_send, v_recv,
    x_send, x_recv, p_send, p_recv,
):
    me_f = lax.axis_index("frame")
    me = lax.axis_index("tensor")
    rows = tok.shape[0]
    width = tok.shape[1]
    cols = wq.shape[1]
    span = keys.shape[0]
    bits = [1 << b for b in range(int(math.log2(frames_n)))][::-1]
    phase_n = len(bits)
    k_order = bits
    v_order = bits[1::-1] + bits[2:] if phase_n > 1 else bits
    n_x = len(edges) - 1
    n_out = width // o_tile
    n_part = width // p_tile
    per_out = o_tile // p_tile
    chained = n_part - direct
    alone = n_part - carry
    has_left = me > 0
    has_right = me < n - 1
    middle = jnp.logical_and(has_left, has_right)
    low_half = 2 * me < n

    q_load = pltpu.make_async_copy(wq_hbm, wq, weight_sem.at[0])
    o_load = pltpu.make_async_copy(wo_hbm, wo, weight_sem.at[1])

    def rows_of(block, count=1):
        return pl.ds(pl.multiple_of(block * rows, rows), count * rows)

    own_x = pltpu.make_async_copy(tok, raw, own_sem)
    own_gain = pltpu.make_async_copy(gain_hbm, gain, small_sem.at[0])
    own_pos = pltpu.make_async_copy(pos_hbm, pos, small_sem.at[1])
    own_pad = pltpu.make_async_copy(pad_hbm, pad, small_sem.at[2])
    own_k = pltpu.make_async_copy(keys, kg.at[pl.ds(0, span)], kv_own.at[0])
    own_v = pltpu.make_async_copy(values, vg.at[pl.ds(0, span)], kv_own.at[1])

    barrier = pltpu.get_barrier_semaphore()
    for bit in bits:
        pl.semaphore_signal(
            barrier, inc=1, device_id={"frame": flip(me_f, bit)}, device_id_type=MESH
        )

    @pl.when(has_left)
    def _():
        pl.semaphore_signal(barrier, inc=1, device_id={"tensor": me - 1}, device_id_type=MESH)

    @pl.when(has_right)
    def _():
        pl.semaphore_signal(barrier, inc=1, device_id={"tensor": me + 1}, device_id_type=MESH)

    own_x.start()
    own_gain.start()
    own_pos.start()
    own_pad.start()
    own_k.start()
    own_v.start()

    own_x.wait()
    own_gain.wait()
    own_k.wait()
    own_v.wait()
    q_load.start()
    o_load.start()
    hidden = raw[...].astype(jnp.float32)
    factor = lax.rsqrt(jnp.mean(hidden * hidden, axis=-1, keepdims=True) + epsilon)
    xg[rows_of(me), :] = (hidden * factor * gain[...]).astype(jnp.bfloat16)
    own_pos.wait()
    own_pad.wait()
    pos_col[...] = jnp.broadcast_to(pos[...], (HEAD_DIM, n * rows)).T

    pl.semaphore_wait(
        barrier, phase_n + has_left.astype(jnp.int32) + has_right.astype(jnp.int32)
    )

    def neighbour(side):
        return lax.rem(me + 1 - 2 * side + n, n)

    def chunk_window(chunk):
        return slice(edges[chunk], edges[chunk + 1])

    def token_copy(block, side, chunk, receiver=None):
        receiver = neighbour(side) if receiver is None else receiver
        window = chunk_window(chunk)
        return pltpu.make_async_remote_copy(
            src_ref=xg.at[rows_of(block), window],
            dst_ref=xg.at[rows_of(block), window],
            send_sem=x_send,
            recv_sem=x_recv.at[block - (block > receiver).astype(jnp.int32), chunk],
            device_id={"tensor": neighbour(side)},
            device_id_type=MESH,
        )

    for chunk in range(n_x):
        @pl.when(has_right)
        def _():
            token_copy(me, 0, chunk).start()

        @pl.when(has_left)
        def _():
            token_copy(me, 1, chunk).start()

    half = cols // 2

    def frame_copy(ref, slot, bit, last, piece, send, recv):
        target = slot + bit
        window = pl.ds(piece * half, half)
        index = target % last + target // (2 * last) * last
        place = recv.at[0] if target & last else recv.at[2 * index - 1 + piece]
        return pltpu.make_async_remote_copy(
            src_ref=ref.at[pl.ds(slot * span, span), window],
            dst_ref=ref.at[pl.ds(target * span, span), window],
            send_sem=send,
            recv_sem=place,
            device_id={"frame": flip(me_f, bit)},
            device_id_type=MESH,
        )

    def plan(ref, order, send, recv):
        steps, held = [], [0]
        last = order[-1]

        def copies(slot, onto):
            return [[frame_copy(ref, slot, bit, last, c, send, recv) for c in range(2)] for bit in onto]

        for p, bit in enumerate(order[:-1]):
            fresh = [slot + bit for slot in held]
            for slot in fresh:
                onward = copies(slot, order[p + 1:])
                for piece, arrival in enumerate(copies(slot - bit, [bit])[0]):
                    steps.append((arrival, [both[piece] for both in onward]))
            held = held + fresh
        own = [copy for both in copies(0, order) for copy in both]
        late = pl.ds(0, len(held) * span)
        rest = pltpu.make_async_remote_copy(
            src_ref=ref.at[late],
            dst_ref=ref.at[late],
            send_sem=send,
            recv_sem=recv.at[0],
            device_id={"frame": flip(me_f, last)},
            device_id_type=MESH,
        )
        return own, steps, rest

    k_own, k_steps, k_rest = plan(kg, k_order, k_send, k_recv)
    v_own, v_steps, v_rest = plan(vg, v_order, v_send, v_recv)
    for pair in zip(k_own, v_own):
        for copy in pair:
            copy.start()
    relays = list(zip(k_steps, v_steps))
    cuts = [0] + [len(relays) * (i + 1) // (n_x + 2) for i in range(n_x)] + [len(relays)]

    def frame_steps(turn):
        for pair in relays[cuts[turn]:cuts[turn + 1]]:
            for arrival, onward in pair:
                arrival.wait_recv()
                for copy in onward:
                    copy.start()

    def frames_done():
        k_rest.wait_recv()
        v_rest.wait_recv()

    slot_of = lax.broadcasted_iota(jnp.int32, (1, span), 1)
    pieces = []
    for slot in range(frames_n):
        owner = me_f
        for bit in bits:
            if slot & bit:
                owner = flip(owner, bit)
        pieces.append(slot_of + owner * span)
    frame_index = jnp.concatenate(pieces, axis=1)
    visible_frames = frame_index < frames_n * span - pad[...]

    scale = HEAD_DIM ** (-0.5)

    def q_step(block, count, place, chunk):
        window = chunk_window(chunk)
        at = rows_of(block, count)
        held = rows_of(place, count)
        product = jnp.dot(xg[at, window], wq[window, :], preferred_element_type=jnp.float32)
        if chunk > 0:
            product = qacc[held, :] + product
        if chunk < n_x - 1:
            qacc[held, :] = product
        else:
            qall[at, :] = (product * scale).astype(jnp.bfloat16)

    def attend(block, count):
        at = rows_of(block, count)
        visible = (frame_index <= pos_col[at, :1]) & visible_frames
        windows = [slice(i, i + HEAD_DIM) for i in range(0, cols, HEAD_DIM)]
        scores = [
            lax.dot_general(
                qall[at, window], kg[:, window], (((1,), (1,)), ((), ())),
                preferred_element_type=jnp.float32,
            )
            for window in windows
        ]
        scores = [jnp.where(visible, score, masked_score) for score in scores]
        highest = [jnp.max(score, axis=-1, keepdims=True) for score in scores]
        weights = [jnp.exp(score - top) for score, top in zip(scores, highest)]
        totals = [jnp.sum(weight, axis=-1, keepdims=True) for weight in weights]
        gathered = [
            jnp.dot(weight.astype(jnp.bfloat16), vg[:, window], preferred_element_type=jnp.float32)
            for weight, window in zip(weights, windows)
        ]
        for window, value, total in zip(windows, gathered, totals):
            abuf[at, window] = (value / total).astype(jnp.bfloat16)

    def part_window(tile):
        return pl.ds(pl.multiple_of(tile * p_tile, p_tile), p_tile)

    def whole_slot(receiver):
        inner = jnp.where(2 * receiver < n, 0, 1)
        return jnp.where(receiver == 0, 1, jnp.where(receiver == n - 1, 0, inner))

    def whole_wait():
        slot = whole_slot(me)
        pltpu.make_async_remote_copy(
            src_ref=pbuf.at[rows_of(me)],
            dst_ref=rbuf.at[slot, rows_of(me)],
            send_sem=p_send,
            recv_sem=p_recv.at[n * n_part],
            device_id={"tensor": neighbour(0)},
            device_id_type=MESH,
        ).wait_recv()

    def part_move(block, side, tile, far, receiver):
        slot = jnp.where(far, 1 - side, side)
        towards = jnp.where(far, block, neighbour(side))
        receiver = towards if receiver is None else receiver
        whole = (block == receiver) & (slot == whole_slot(receiver))
        return pltpu.make_async_remote_copy(
            src_ref=pbuf.at[rows_of(block), part_window(tile)],
            dst_ref=rbuf.at[slot, rows_of(block), part_window(tile)],
            send_sem=p_send,
            recv_sem=p_recv.at[jnp.where(whole, n * n_part, block * n_part + tile)],
            device_id={"tensor": towards},
            device_id_type=MESH,
        )

    def part_copy(block, side, tile, far=False):
        return part_move(block, side, tile, far, None)

    def part_here(block, side, tile):
        return part_move(block, side, tile, False, me)

    def project(block, count, first_tile, send):
        at = rows_of(block, count)

        def body(index, _):
            tile = lax.rem(index + first_tile, n_out)
            window = pl.ds(pl.multiple_of(tile * o_tile, o_tile), o_tile)
            pbuf[at, window] = jnp.dot(
                abuf[at, :], wo[:, window], preferred_element_type=jnp.float32
            ).astype(jnp.bfloat16)

            if send is not None:
                send(tile)
            return 0

        lax.fori_loop(0, n_out, body, 0)

    def add_part(block, side, tile):
        at = rows_of(block)
        window = part_window(tile)
        part_here(block, side, tile).wait_recv()
        pbuf[at, window] = (
            pbuf[at, window].astype(jnp.float32) + rbuf[side, at, window].astype(jnp.float32)
        ).astype(jnp.bfloat16)

    def parts_of(tile):
        return [tile * per_out + part for part in range(per_out)]

    def drain_inputs():
        def drain_tokens(count):
            sent = pl.ds(0, count * rows)
            pltpu.make_async_remote_copy(
                src_ref=xg.at[sent],
                dst_ref=xg.at[sent],
                send_sem=x_send,
                recv_sem=x_recv.at[0, 0],
                device_id={"tensor": neighbour(0)},
                device_id_type=MESH,
            ).wait_send()

        @pl.when(middle)
        def _():
            drain_tokens(n + 1)

        @pl.when(jnp.logical_not(middle))
        def _():
            drain_tokens(1)

        others = pl.ds(0, (frames_n - 1) * span)
        for ref, send, recv in ((kg, k_send, k_recv), (vg, v_send, v_recv)):
            pltpu.make_async_remote_copy(
                src_ref=ref.at[others],
                dst_ref=ref.at[others],
                send_sem=send,
                recv_sem=recv.at[0],
                device_id={"frame": flip(me_f, bits[0])},
                device_id_type=MESH,
            ).wait_send()

    @pl.when(jnp.logical_not(middle))
    def _():
        heading = jnp.where(has_left, -1, 1)
        arriving = jnp.where(has_left, 0, 1)
        leaving = 1 - arriving
        near = me + heading
        first = jnp.minimum(me, near)
        frame_steps(0)
        q_load.wait()
        for chunk in range(n_x):
            token_copy(near, arriving, chunk, me).wait_recv()
            q_step(first, 2, 0, chunk)
            frame_steps(chunk + 1)
        frames_done()
        attend(near, 1)
        o_load.wait()

        def send_near(tile):
            for part in parts_of(tile):
                @pl.when(part < n_part - defer)
                def _():
                    part_copy(near, leaving, part).start()

        project(near, 1, 0, send_near)

        def stage_body(stage, _):
            block = me + heading * stage

            for chunk in range(n_x):
                token_copy(block, arriving, chunk, me).wait_recv()
                q_step(block, 1, 0, chunk)
            attend(block, 1)

            def send_block(tile):
                for part in parts_of(tile):
                    far = jnp.logical_and(stage == n - 1, part >= chained)

                    @pl.when(far & has_left & (part >= alone))
                    def _():
                        add_part(block, 0, part)

                    part_copy(block, leaving, part, far).start()

            project(block, 1, 0, send_block)
            return 0

        lax.fori_loop(2, n, stage_body, 0)
        for part in range(n_part - defer, n_part):
            part_copy(near, leaving, part).start()
        attend(me, 1)
        project(me, 1, 0, None)
        drain_inputs()

        whole_wait()

        def sum_body(tile, _):
            window = part_window(tile)
            total = pbuf[rows_of(me), window].astype(jnp.float32)
            total = total + rbuf[arriving, rows_of(me), window].astype(jnp.float32)

            @pl.when(tile < chained)
            def _():
                out[:, window] = total.astype(jnp.bfloat16)

            @pl.when(tile >= chained)
            def _():
                part_here(me, leaving, tile).wait_recv()
                straight = rbuf[leaving, rows_of(me), window].astype(jnp.float32)
                out[:, window] = (total + straight).astype(jnp.bfloat16)

            return 0

        def sum_index(index, _):
            return sum_body(lax.rem(index + chained, n_part), 0)

        lax.fori_loop(0, n_part, sum_index, 0)

    @pl.when(middle)
    def _():
        frame_steps(0)
        q_load.wait()
        for chunk in range(n_x):
            for side, block in ((0, me - 1), (1, me + 1)):
                token_copy(block, side, chunk, me).wait_recv()
                token_copy(block, side, chunk).start()
            q_step(me - 1, 3, 0, chunk)
            frame_steps(chunk + 1)

        def near_attend():
            frames_done()
            attend(me - 1, 3)

        def stage_body(stage, _):
            for chunk in range(n_x):
                def side_body(side, _):
                    block = me - stage + 2 * side * stage

                    @pl.when(jnp.logical_and(block >= 0, block < n))
                    def _():
                        token_copy(block, side, chunk, me).wait_recv()
                        token_copy(block, side, chunk).start()
                        q_step(block, 1, side, chunk)

                    return 0

                lax.fori_loop(0, 2, side_body, 0)
                if chunk == 0:
                    pl.when(stage == 2)(near_attend)

            def attend_body(side, _):
                block = me - stage + 2 * side * stage

                @pl.when(jnp.logical_and(block >= 0, block < n))
                def _():
                    attend(block, 1)

                return 0

            lax.fori_loop(0, 2, attend_body, 0)
            return 0

        if n == 3:
            near_attend()
        lax.fori_loop(2, n - 1, stage_body, 0)
        groups = max(1, n * rows // HEAD_DIM)
        while n % groups:
            groups -= 1
        count = n // groups
        o_load.wait()

        def group_body(group, _):
            def send_started(tile):
                last = group == groups - 1
                for part in parts_of(tile):
                    @pl.when((me == 1) & last & (part >= chained))
                    def _():
                        part_copy(n - 1, 0, part).start()

                    carried = part >= alone
                    begins = jnp.where(carried, me == n - 3, me == n - 2)

                    @pl.when(begins & (group == 0) & (part >= chained))
                    def _():
                        part_copy(0, 1, part).start()

            project(group * count, count, chained // per_out % n_out, send_started)
            return 0

        lax.fori_loop(0, groups, group_body, 0)

        @pl.when(me == n - 2)
        def _():
            for part in range(alone, n_part):
                part_copy(0, 0, part).start()

        def relay(block, side, tile):
            add_part(block, side, tile)
            part_copy(block, side, tile).start()

        def relay_body(index, _):
            def side_body(turn, _):
                side = jnp.where(low_half, turn, 1 - turn)
                at = index - turn * lag
                stage = 1 + lax.div(jnp.maximum(at, 0), n_part)
                tile = lax.rem(jnp.maximum(at, 0), n_part)
                block = jnp.where(side == 0, stage, n - 1 - stage)
                passes = jnp.where(side == 0, block > me, block < me)
                chain = (stage < n - 1) | ((stage == n - 1) & (tile < chained))

                @pl.when((at >= 0) & chain & passes)
                def _():
                    relay(block, side, tile)

                far = index - (n - 3) * n_part - early
                carried = chained + far >= alone
                beside = jnp.where(side == 0, me == 1, (me == n - 2) | (carried & (me == n - 3)))

                @pl.when((far >= 0) & (far < direct) & jnp.logical_not(beside))
                def _():
                    relay(jnp.where(side == 0, n - 1, 0), side, chained + far)

                return 0

            lax.fori_loop(0, 2, side_body, 0)
            return 0

        behind = jnp.minimum(me, n - 1 - me) * n_part
        lax.fori_loop(jnp.minimum(behind, (n - 3) * n_part + early), (n - 1) * n_part + lag, relay_body, 0)

        whole_wait()
        slot = whole_slot(me)

        def sum_body(tile, _):
            window = part_window(tile)
            part_here(me, 1 - slot, tile).wait_recv()
            total = pbuf[rows_of(me), window].astype(jnp.float32)
            for side in range(2):
                total = total + rbuf[side, rows_of(me), window].astype(jnp.float32)
            out[:, window] = total.astype(jnp.bfloat16)
            return 0

        lax.fori_loop(0, n_part, sum_body, 0)
        drain_inputs()

    others = pl.ds(0, (n - 1) * rows)
    pltpu.make_async_remote_copy(
        src_ref=pbuf.at[others],
        dst_ref=rbuf.at[0, others],
        send_sem=p_send,
        recv_sem=p_recv.at[0],
        device_id={"tensor": neighbour(0)},
        device_id_type=MESH,
    ).wait_send()


def divisor(total, most):
    return math.gcd(total, most)


def per_device(
    n, frames_n,
    tokens, norm_gain, query_weight, out_weight, cache_keys, cache_values, token_pos, frame_pad
):
    rows, seqs, width = tokens.shape
    cols = query_weight.shape[1]
    span = cache_keys.shape[0]
    unit = divisor(width, 256)
    shares = (6, 5, 3, 2)
    edges = [width // unit * sum(shares[:i]) // sum(shares) * unit for i in range(len(shares) + 1)]
    o_tile = divisor(width, 512)
    p_tile = divisor(o_tile, 512)
    n_x = len(shares)
    n_part = width // p_tile
    lag = max(1, 5 * n_part // 8)
    direct = n_part if n > 2 else 0
    early = -(2 * n_part // 8)
    carry = 3 * n_part // 8 if n > 3 else 0
    defer = n_part // 8 if n > 3 else 0
    hbm = pl.BlockSpec(memory_space=pltpu.HBM)
    vmem = pl.BlockSpec(memory_space=pltpu.VMEM)
    bf16 = jnp.bfloat16
    dma = pltpu.SemaphoreType.DMA
    result = pl.pallas_call(
        functools.partial(kernel, n, frames_n, edges, o_tile, p_tile, lag, direct, early, carry, defer),
        out_shape=pltpu.VMEM((rows, width), bf16),
        in_specs=[hbm] * 8,
        out_specs=vmem,
        scratch_shapes=[
            pltpu.VMEM(query_weight.shape, bf16),
            pltpu.VMEM(out_weight.shape, bf16),
            pltpu.VMEM((frames_n * span, cols), bf16),
            pltpu.VMEM((frames_n * span, cols), bf16),
            pltpu.VMEM((n * rows, HEAD_DIM), jnp.int32),
            pltpu.VMEM((1, width), jnp.float32),
            pltpu.VMEM((1, n * rows), jnp.int32),
            pltpu.VMEM((1, 1), jnp.int32),
            pltpu.VMEM((rows, width), bf16),
            pltpu.VMEM(((n + 1) * rows, width), bf16),
            pltpu.VMEM((3 * rows, cols), jnp.float32),
            pltpu.VMEM((n * rows, cols), bf16),
            pltpu.VMEM((n * rows, cols), bf16),
            pltpu.VMEM((n * rows, width), bf16),
            pltpu.VMEM((2, n * rows, width), bf16),
            dma((2,)),
            dma(()),
            dma((3,)),
            dma((2,)),
            dma(()),
            dma((frames_n - 1,)),
            dma(()),
            dma((frames_n - 1,)),
            dma(()),
            dma((n - 1, n_x)),
            dma(()),
            dma((n * n_part + 1,)),
        ],
        compiler_params=pltpu.CompilerParams(collective_id=0, has_side_effects=True),
    )(
        tokens.reshape(rows, width),
        norm_gain.reshape(1, width),
        query_weight,
        out_weight,
        cache_keys.reshape(span, cols),
        cache_values.reshape(span, cols),
        token_pos.reshape(1, n * rows),
        frame_pad.reshape(1, 1),
    )
    return result.reshape(rows, seqs, width)


def solution(mesh):
    placed = (
        P(("frame", "tensor"), None, None),
        P(),
        P(None, "tensor"),
        P("tensor", None),
        P("frame", None, "tensor"),
        P("frame", None, "tensor"),
        P("frame", None),
        P(),
    )
    return jax.shard_map(
        functools.partial(per_device, mesh.shape["tensor"], mesh.shape["frame"]),
        mesh=mesh,
        in_specs=placed,
        out_specs=P(("frame", "tensor"), None, None),
        check_vma=False,
    )
```

```python
import functools
import math

import jax
import jax.numpy as jnp
from jax import lax
from jax.experimental import pallas as pl
from jax.experimental.pallas import tpu as pltpu
from jax.sharding import PartitionSpec as P

HEAD_DIM = 128
epsilon = 1e-06
masked_score = -1e30
MESH = pl.DeviceIdType.MESH


def flip(index, bit):
    return index + bit - 2 * bit * lax.rem(lax.div(index, bit), 2)


def kernel(
    n, frames_n, edges, o_tile, p_tile, lag, direct, early, carry, defer,
    tok, gain_hbm, wq_hbm, wo_hbm, keys, values, pos_hbm, pad_hbm,
    out,
    wq, wo, kg, vg, pos_col, gain, pos, pad, raw, xg, qacc, qall, abuf, pbuf, rbuf,
    weight_sem, own_sem, small_sem, kv_own, k_send, k_recv, v_send, v_recv,
    x_send, x_recv, p_send, p_recv,
):
    me_f = lax.axis_index("frame")
    me = lax.axis_index("tensor")
    rows = tok.shape[0]
    width = tok.shape[1]
    cols = wq.shape[1]
    span = keys.shape[0]
    bits = [1 << b for b in range(int(math.log2(frames_n)))][::-1]
    phase_n = len(bits)
    k_order = bits
    v_order = bits[1::-1] + bits[2:] if phase_n > 1 else bits
    n_x = len(edges) - 1
    n_out = width // o_tile
    n_part = width // p_tile
    per_out = o_tile // p_tile
    chained = n_part - direct
    alone = n_part - carry
    has_left = me > 0
    has_right = me < n - 1
    middle = jnp.logical_and(has_left, has_right)
    low_half = 2 * me < n

    q_load = pltpu.make_async_copy(wq_hbm, wq, weight_sem.at[0])
    o_load = pltpu.make_async_copy(wo_hbm, wo, weight_sem.at[1])

    def rows_of(block, count=1):
        return pl.ds(pl.multiple_of(block * rows, rows), count * rows)

    own_x = pltpu.make_async_copy(tok, raw, own_sem)
    own_gain = pltpu.make_async_copy(gain_hbm, gain, small_sem.at[0])
    own_pos = pltpu.make_async_copy(pos_hbm, pos, small_sem.at[1])
    own_pad = pltpu.make_async_copy(pad_hbm, pad, small_sem.at[2])
    own_k = pltpu.make_async_copy(keys, kg.at[pl.ds(0, span)], kv_own.at[0])
    own_v = pltpu.make_async_copy(values, vg.at[pl.ds(0, span)], kv_own.at[1])

    barrier = pltpu.get_barrier_semaphore()
    for bit in bits:
        pl.semaphore_signal(
            barrier, inc=1, device_id={"frame": flip(me_f, bit)}, device_id_type=MESH
        )

    @pl.when(has_left)
    def _():
        pl.semaphore_signal(barrier, inc=1, device_id={"tensor": me - 1}, device_id_type=MESH)

    @pl.when(has_right)
    def _():
        pl.semaphore_signal(barrier, inc=1, device_id={"tensor": me + 1}, device_id_type=MESH)

    own_x.start()
    own_gain.start()
    own_pos.start()
    own_pad.start()
    own_k.start()
    own_v.start()

    own_x.wait()
    own_gain.wait()
    own_k.wait()
    own_v.wait()
    q_load.start()
    o_load.start()
    hidden = raw[...].astype(jnp.float32)
    factor = lax.rsqrt(jnp.mean(hidden * hidden, axis=-1, keepdims=True) + epsilon)
    xg[rows_of(me), :] = (hidden * factor * gain[...]).astype(jnp.bfloat16)
    own_pos.wait()
    own_pad.wait()
    pos_col[...] = jnp.broadcast_to(pos[...], (HEAD_DIM, n * rows)).T

    pl.semaphore_wait(
        barrier, phase_n + has_left.astype(jnp.int32) + has_right.astype(jnp.int32)
    )

    def neighbour(side):
        return lax.rem(me + 1 - 2 * side + n, n)

    def chunk_window(chunk):
        return slice(edges[chunk], edges[chunk + 1])

    def token_copy(block, side, chunk, receiver=None):
        receiver = neighbour(side) if receiver is None else receiver
        window = chunk_window(chunk)
        return pltpu.make_async_remote_copy(
            src_ref=xg.at[rows_of(block), window],
            dst_ref=xg.at[rows_of(block), window],
            send_sem=x_send,
            recv_sem=x_recv.at[block - (block > receiver).astype(jnp.int32), chunk],
            device_id={"tensor": neighbour(side)},
            device_id_type=MESH,
        )

    half = cols // 2

    def frame_copy(ref, slot, bit, last, piece, send, recv):
        target = slot + bit
        window = pl.ds(piece * half, half)
        index = target % last + target // (2 * last) * last
        place = recv.at[0] if target & last else recv.at[2 * index - 1 + piece]
        return pltpu.make_async_remote_copy(
            src_ref=ref.at[pl.ds(slot * span, span), window],
            dst_ref=ref.at[pl.ds(target * span, span), window],
            send_sem=send,
            recv_sem=place,
            device_id={"frame": flip(me_f, bit)},
            device_id_type=MESH,
        )

    def plan(ref, order, send, recv):
        steps, held = [], [0]
        last = order[-1]

        def copies(slot, onto):
            return [[frame_copy(ref, slot, bit, last, c, send, recv) for c in range(2)] for bit in onto]

        for p, bit in enumerate(order[:-1]):
            fresh = [slot + bit for slot in held]
            for slot in fresh:
                onward = copies(slot, order[p + 1:])
                for piece, arrival in enumerate(copies(slot - bit, [bit])[0]):
                    steps.append((arrival, [both[piece] for both in onward]))
            held = held + fresh
        own = [copy for both in copies(0, order) for copy in both]
        late = pl.ds(0, len(held) * span)
        rest = pltpu.make_async_remote_copy(
            src_ref=ref.at[late],
            dst_ref=ref.at[late],
            send_sem=send,
            recv_sem=recv.at[0],
            device_id={"frame": flip(me_f, last)},
            device_id_type=MESH,
        )
        return own, steps, rest

    k_own, k_steps, k_rest = plan(kg, k_order, k_send, k_recv)
    v_own, v_steps, v_rest = plan(vg, v_order, v_send, v_recv)
    for pair in zip(k_own, v_own):
        for copy in pair:
            copy.start()
    for chunk in range(n_x):
        @pl.when(has_right)
        def _():
            token_copy(me, 0, chunk).start()

        @pl.when(has_left)
        def _():
            token_copy(me, 1, chunk).start()

    relays = list(zip(k_steps, v_steps))
    cuts = [0] + [len(relays) * (i + 1) // (n_x + 2) for i in range(n_x)] + [len(relays)]

    def frame_steps(turn):
        for pair in relays[cuts[turn]:cuts[turn + 1]]:
            for arrival, onward in pair:
                arrival.wait_recv()
                for copy in onward:
                    copy.start()

    def frames_done():
        k_rest.wait_recv()
        v_rest.wait_recv()

    slot_of = lax.broadcasted_iota(jnp.int32, (1, span), 1)
    pieces = []
    for slot in range(frames_n):
        owner = me_f
        for bit in bits:
            if slot & bit:
                owner = flip(owner, bit)
        pieces.append(slot_of + owner * span)
    frame_index = jnp.concatenate(pieces, axis=1)
    visible_frames = frame_index < frames_n * span - pad[...]

    scale = HEAD_DIM ** (-0.5)

    def q_step(block, count, place, chunk):
        window = chunk_window(chunk)
        at = rows_of(block, count)
        held = rows_of(place, count)
        product = jnp.dot(xg[at, window], wq[window, :], preferred_element_type=jnp.float32)
        if chunk > 0:
            product = qacc[held, :] + product
        if chunk < n_x - 1:
            qacc[held, :] = product
        else:
            qall[at, :] = (product * scale).astype(jnp.bfloat16)

    def attend(block, count):
        at = rows_of(block, count)
        visible = (frame_index <= pos_col[at, :1]) & visible_frames
        windows = [slice(i, i + HEAD_DIM) for i in range(0, cols, HEAD_DIM)]
        scores = [
            lax.dot_general(
                qall[at, window], kg[:, window], (((1,), (1,)), ((), ())),
                preferred_element_type=jnp.float32,
            )
            for window in windows
        ]
        scores = [jnp.where(visible, score, masked_score) for score in scores]
        highest = [jnp.max(score, axis=-1, keepdims=True) for score in scores]
        weights = [jnp.exp(score - top) for score, top in zip(scores, highest)]
        totals = [jnp.sum(weight, axis=-1, keepdims=True) for weight in weights]
        gathered = [
            jnp.dot(weight.astype(jnp.bfloat16), vg[:, window], preferred_element_type=jnp.float32)
            for weight, window in zip(weights, windows)
        ]
        for window, value, total in zip(windows, gathered, totals):
            abuf[at, window] = (value / total).astype(jnp.bfloat16)

    def part_window(tile):
        return pl.ds(pl.multiple_of(tile * p_tile, p_tile), p_tile)

    def whole_slot(receiver):
        inner = jnp.where(2 * receiver < n, 0, 1)
        return jnp.where(receiver == 0, 1, jnp.where(receiver == n - 1, 0, inner))

    def whole_wait():
        slot = whole_slot(me)
        pltpu.make_async_remote_copy(
            src_ref=pbuf.at[rows_of(me)],
            dst_ref=rbuf.at[slot, rows_of(me)],
            send_sem=p_send,
            recv_sem=p_recv.at[n * n_part],
            device_id={"tensor": neighbour(0)},
            device_id_type=MESH,
        ).wait_recv()

    def part_move(block, side, tile, far, receiver):
        slot = jnp.where(far, 1 - side, side)
        towards = jnp.where(far, block, neighbour(side))
        receiver = towards if receiver is None else receiver
        whole = (block == receiver) & (slot == whole_slot(receiver))
        return pltpu.make_async_remote_copy(
            src_ref=pbuf.at[rows_of(block), part_window(tile)],
            dst_ref=rbuf.at[slot, rows_of(block), part_window(tile)],
            send_sem=p_send,
            recv_sem=p_recv.at[jnp.where(whole, n * n_part, block * n_part + tile)],
            device_id={"tensor": towards},
            device_id_type=MESH,
        )

    def part_copy(block, side, tile, far=False):
        return part_move(block, side, tile, far, None)

    def part_here(block, side, tile):
        return part_move(block, side, tile, False, me)

    def project(block, count, first_tile, send):
        at = rows_of(block, count)

        def body(index, _):
            tile = lax.rem(index + first_tile, n_out)
            window = pl.ds(pl.multiple_of(tile * o_tile, o_tile), o_tile)
            pbuf[at, window] = jnp.dot(
                abuf[at, :], wo[:, window], preferred_element_type=jnp.float32
            ).astype(jnp.bfloat16)

            if send is not None:
                send(tile)
            return 0

        lax.fori_loop(0, n_out, body, 0)

    def add_part(block, side, tile):
        at = rows_of(block)
        window = part_window(tile)
        part_here(block, side, tile).wait_recv()
        pbuf[at, window] = (
            pbuf[at, window].astype(jnp.float32) + rbuf[side, at, window].astype(jnp.float32)
        ).astype(jnp.bfloat16)

    def parts_of(tile):
        return [tile * per_out + part for part in range(per_out)]

    def drain_inputs():
        def drain_tokens(count):
            sent = pl.ds(0, count * rows)
            pltpu.make_async_remote_copy(
                src_ref=xg.at[sent],
                dst_ref=xg.at[sent],
                send_sem=x_send,
                recv_sem=x_recv.at[0, 0],
                device_id={"tensor": neighbour(0)},
                device_id_type=MESH,
            ).wait_send()

        @pl.when(middle)
        def _():
            drain_tokens(n + 1)

        @pl.when(jnp.logical_not(middle))
        def _():
            drain_tokens(1)

        others = pl.ds(0, (frames_n - 1) * span)
        for ref, send, recv in ((kg, k_send, k_recv), (vg, v_send, v_recv)):
            pltpu.make_async_remote_copy(
                src_ref=ref.at[others],
                dst_ref=ref.at[others],
                send_sem=send,
                recv_sem=recv.at[0],
                device_id={"frame": flip(me_f, bits[0])},
                device_id_type=MESH,
            ).wait_send()

    @pl.when(jnp.logical_not(middle))
    def _():
        heading = jnp.where(has_left, -1, 1)
        arriving = jnp.where(has_left, 0, 1)
        leaving = 1 - arriving
        near = me + heading
        first = jnp.minimum(me, near)
        frame_steps(0)
        q_load.wait()
        for chunk in range(n_x):
            token_copy(near, arriving, chunk, me).wait_recv()
            q_step(first, 2, 0, chunk)
            frame_steps(chunk + 1)
        frames_done()
        attend(near, 1)
        o_load.wait()

        def send_near(tile):
            for part in parts_of(tile):
                @pl.when(part < n_part - defer)
                def _():
                    part_copy(near, leaving, part).start()

        project(near, 1, 0, send_near)

        def stage_body(stage, _):
            block = me + heading * stage

            for chunk in range(n_x):
                token_copy(block, arriving, chunk, me).wait_recv()
                q_step(block, 1, 0, chunk)
            attend(block, 1)

            def send_block(tile):
                for part in parts_of(tile):
                    far = jnp.logical_and(stage == n - 1, part >= chained)

                    @pl.when(far & has_left & (part >= alone))
                    def _():
                        add_part(block, 0, part)

                    part_copy(block, leaving, part, far).start()

            project(block, 1, 0, send_block)
            return 0

        lax.fori_loop(2, n, stage_body, 0)
        for part in range(n_part - defer, n_part):
            part_copy(near, leaving, part).start()
        attend(me, 1)
        project(me, 1, 0, None)
        drain_inputs()

        whole_wait()

        def sum_body(tile, _):
            window = part_window(tile)
            total = pbuf[rows_of(me), window].astype(jnp.float32)
            total = total + rbuf[arriving, rows_of(me), window].astype(jnp.float32)

            @pl.when(tile < chained)
            def _():
                out[:, window] = total.astype(jnp.bfloat16)

            @pl.when(tile >= chained)
            def _():
                part_here(me, leaving, tile).wait_recv()
                straight = rbuf[leaving, rows_of(me), window].astype(jnp.float32)
                out[:, window] = (total + straight).astype(jnp.bfloat16)

            return 0

        def sum_index(index, _):
            return sum_body(lax.rem(index + chained, n_part), 0)

        lax.fori_loop(0, n_part, sum_index, 0)

    @pl.when(middle)
    def _():
        frame_steps(0)
        q_load.wait()
        for chunk in range(n_x):
            for side, block in ((0, me - 1), (1, me + 1)):
                token_copy(block, side, chunk, me).wait_recv()
                token_copy(block, side, chunk).start()
            q_step(me - 1, 3, 0, chunk)
            frame_steps(chunk + 1)

        def near_attend():
            frames_done()
            attend(me - 1, 3)

        def stage_body(stage, _):
            for chunk in range(n_x):
                def side_body(side, _):
                    block = me - stage + 2 * side * stage

                    @pl.when(jnp.logical_and(block >= 0, block < n))
                    def _():
                        token_copy(block, side, chunk, me).wait_recv()
                        token_copy(block, side, chunk).start()
                        q_step(block, 1, side, chunk)

                    return 0

                lax.fori_loop(0, 2, side_body, 0)
                if chunk == 0:
                    pl.when(stage == 2)(near_attend)

            def attend_body(side, _):
                block = me - stage + 2 * side * stage

                @pl.when(jnp.logical_and(block >= 0, block < n))
                def _():
                    attend(block, 1)

                return 0

            lax.fori_loop(0, 2, attend_body, 0)
            return 0

        if n == 3:
            near_attend()
        lax.fori_loop(2, n - 1, stage_body, 0)
        groups = max(1, n * rows // HEAD_DIM)
        while n % groups:
            groups -= 1
        count = n // groups
        o_load.wait()

        def group_body(group, _):
            def send_started(tile):
                last = group == groups - 1
                for part in parts_of(tile):
                    @pl.when((me == 1) & last & (part >= chained))
                    def _():
                        part_copy(n - 1, 0, part).start()


                    @pl.when((me == n - 2) & (group == 0) & (part >= chained) & (part < alone))
                    def _():
                        part_copy(0, 1, part).start()

            project(group * count, count, chained // per_out % n_out, send_started)
            return 0

        lax.fori_loop(0, groups, group_body, 0)

        @pl.when(me == n - 2)
        def _():
            for part in range(alone, n_part):
                part_copy(0, 0, part).start()

        @pl.when(me == n - 3)
        def _():
            for part in range(alone, n_part):
                part_copy(0, 1, part).start()

        def relay(block, side, tile):
            add_part(block, side, tile)
            part_copy(block, side, tile).start()

        def relay_body(index, _):
            def side_body(turn, _):
                side = jnp.where(low_half, turn, 1 - turn)
                at = index - turn * lag
                stage = 1 + lax.div(jnp.maximum(at, 0), n_part)
                tile = lax.rem(jnp.maximum(at, 0), n_part)
                block = jnp.where(side == 0, stage, n - 1 - stage)
                passes = jnp.where(side == 0, block > me, block < me)
                chain = (stage < n - 1) | ((stage == n - 1) & (tile < chained))

                @pl.when((at >= 0) & chain & passes)
                def _():
                    relay(block, side, tile)

                far = index - (n - 3) * n_part - early
                carried = chained + far >= alone
                beside = jnp.where(side == 0, me == 1, (me == n - 2) | (carried & (me == n - 3)))

                @pl.when((far >= 0) & (far < direct) & jnp.logical_not(beside))
                def _():
                    relay(jnp.where(side == 0, n - 1, 0), side, chained + far)

                return 0

            lax.fori_loop(0, 2, side_body, 0)
            return 0

        behind = jnp.minimum(me, n - 1 - me) * n_part
        lax.fori_loop(jnp.minimum(behind, (n - 3) * n_part + early), (n - 1) * n_part + lag, relay_body, 0)

        whole_wait()
        slot = whole_slot(me)

        def sum_body(tile, _):
            window = part_window(tile)
            part_here(me, 1 - slot, tile).wait_recv()
            total = pbuf[rows_of(me), window].astype(jnp.float32)
            for side in range(2):
                total = total + rbuf[side, rows_of(me), window].astype(jnp.float32)
            out[:, window] = total.astype(jnp.bfloat16)
            return 0

        lax.fori_loop(0, n_part, sum_body, 0)
        drain_inputs()

    others = pl.ds(0, (n - 1) * rows)
    pltpu.make_async_remote_copy(
        src_ref=pbuf.at[others],
        dst_ref=rbuf.at[0, others],
        send_sem=p_send,
        recv_sem=p_recv.at[0],
        device_id={"tensor": neighbour(0)},
        device_id_type=MESH,
    ).wait_send()


def divisor(total, most):
    return math.gcd(total, most)


def per_device(
    n, frames_n,
    tokens, norm_gain, query_weight, out_weight, cache_keys, cache_values, token_pos, frame_pad
):
    rows, seqs, width = tokens.shape
    cols = query_weight.shape[1]
    span = cache_keys.shape[0]
    unit = divisor(width, 256)
    shares = (5, 5, 4, 2)
    edges = [width // unit * sum(shares[:i]) // sum(shares) * unit for i in range(len(shares) + 1)]
    o_tile = divisor(width, 512)
    p_tile = divisor(o_tile, 512)
    n_x = len(shares)
    n_part = width // p_tile
    lag = max(1, 5 * n_part // 8)
    direct = n_part if n > 2 else 0
    early = -(2 * n_part // 8)
    carry = 3 * n_part // 8 if n > 3 else 0
    defer = n_part // 8 if n > 3 else 0
    hbm = pl.BlockSpec(memory_space=pltpu.HBM)
    vmem = pl.BlockSpec(memory_space=pltpu.VMEM)
    bf16 = jnp.bfloat16
    dma = pltpu.SemaphoreType.DMA
    result = pl.pallas_call(
        functools.partial(kernel, n, frames_n, edges, o_tile, p_tile, lag, direct, early, carry, defer),
        out_shape=pltpu.VMEM((rows, width), bf16),
        in_specs=[hbm] * 8,
        out_specs=vmem,
        scratch_shapes=[
            pltpu.VMEM(query_weight.shape, bf16),
            pltpu.VMEM(out_weight.shape, bf16),
            pltpu.VMEM((frames_n * span, cols), bf16),
            pltpu.VMEM((frames_n * span, cols), bf16),
            pltpu.VMEM((n * rows, HEAD_DIM), jnp.int32),
            pltpu.VMEM((1, width), jnp.float32),
            pltpu.VMEM((1, n * rows), jnp.int32),
            pltpu.VMEM((1, 1), jnp.int32),
            pltpu.VMEM((rows, width), bf16),
            pltpu.VMEM(((n + 1) * rows, width), bf16),
            pltpu.VMEM((3 * rows, cols), jnp.float32),
            pltpu.VMEM((n * rows, cols), bf16),
            pltpu.VMEM((n * rows, cols), bf16),
            pltpu.VMEM((n * rows, width), bf16),
            pltpu.VMEM((2, n * rows, width), bf16),
            dma((2,)),
            dma(()),
            dma((3,)),
            dma((2,)),
            dma(()),
            dma((frames_n - 1,)),
            dma(()),
            dma((frames_n - 1,)),
            dma(()),
            dma((n - 1, n_x)),
            dma(()),
            dma((n * n_part + 1,)),
        ],
        compiler_params=pltpu.CompilerParams(collective_id=0, has_side_effects=True),
    )(
        tokens.reshape(rows, width),
        norm_gain.reshape(1, width),
        query_weight,
        out_weight,
        cache_keys.reshape(span, cols),
        cache_values.reshape(span, cols),
        token_pos.reshape(1, n * rows),
        frame_pad.reshape(1, 1),
    )
    return result.reshape(rows, seqs, width)


def solution(mesh):
    placed = (
        P(("frame", "tensor"), None, None),
        P(),
        P(None, "tensor"),
        P("tensor", None),
        P("frame", None, "tensor"),
        P("frame", None, "tensor"),
        P("frame", None),
        P(),
    )
    return jax.shard_map(
        functools.partial(per_device, mesh.shape["tensor"], mesh.shape["frame"]),
        mesh=mesh,
        in_specs=placed,
        out_specs=P(("frame", "tensor"), None, None),
        check_vma=False,
    )
```

```python
import functools
import math

import jax
import jax.numpy as jnp
from jax import lax
from jax.experimental import pallas as pl
from jax.experimental.pallas import tpu as pltpu
from jax.sharding import PartitionSpec as P

HEAD_DIM = 128
epsilon = 1e-06
masked_score = -1e30
MESH = pl.DeviceIdType.MESH


def flip(index, bit):
    return index + bit - 2 * bit * lax.rem(lax.div(index, bit), 2)


def kernel(
    n, frames_n, edges, o_tile, p_tile, lag, direct, early, carry, defer,
    tok, gain_hbm, wq_hbm, wo_hbm, keys, values, pos_hbm, pad_hbm,
    out,
    wq, wo, kg, vg, pos_col, gain, pos, pad, raw, xg, qacc, qall, abuf, pbuf, rbuf,
    weight_sem, own_sem, small_sem, kv_own, k_send, k_recv, v_send, v_recv,
    x_send, x_recv, p_send, p_recv,
):
    me_f = lax.axis_index("frame")
    me = lax.axis_index("tensor")
    rows = tok.shape[0]
    width = tok.shape[1]
    cols = wq.shape[1]
    span = keys.shape[0]
    bits = [1 << b for b in range(int(math.log2(frames_n)))][::-1]
    phase_n = len(bits)
    k_order = bits
    v_order = bits[1::-1] + bits[2:] if phase_n > 1 else bits
    n_x = len(edges) - 1
    n_out = width // o_tile
    n_part = width // p_tile
    per_out = o_tile // p_tile
    chained = n_part - direct
    alone = n_part - carry
    has_left = me > 0
    has_right = me < n - 1
    middle = jnp.logical_and(has_left, has_right)
    low_half = 2 * me < n

    q_load = pltpu.make_async_copy(wq_hbm, wq, weight_sem.at[0])
    o_load = pltpu.make_async_copy(wo_hbm, wo, weight_sem.at[1])

    def rows_of(block, count=1):
        return pl.ds(pl.multiple_of(block * rows, rows), count * rows)

    own_x = pltpu.make_async_copy(tok, raw, own_sem)
    own_gain = pltpu.make_async_copy(gain_hbm, gain, small_sem.at[0])
    own_pos = pltpu.make_async_copy(pos_hbm, pos, small_sem.at[1])
    own_pad = pltpu.make_async_copy(pad_hbm, pad, small_sem.at[2])
    own_k = pltpu.make_async_copy(keys, kg.at[pl.ds(0, span)], kv_own.at[0])
    own_v = pltpu.make_async_copy(values, vg.at[pl.ds(0, span)], kv_own.at[1])

    barrier = pltpu.get_barrier_semaphore()
    for bit in bits:
        pl.semaphore_signal(
            barrier, inc=1, device_id={"frame": flip(me_f, bit)}, device_id_type=MESH
        )

    @pl.when(has_left)
    def _():
        pl.semaphore_signal(barrier, inc=1, device_id={"tensor": me - 1}, device_id_type=MESH)

    @pl.when(has_right)
    def _():
        pl.semaphore_signal(barrier, inc=1, device_id={"tensor": me + 1}, device_id_type=MESH)

    own_x.start()
    own_gain.start()
    own_pos.start()
    own_pad.start()
    own_k.start()
    own_v.start()

    own_x.wait()
    own_gain.wait()
    own_k.wait()
    own_v.wait()
    q_load.start()
    o_load.start()
    hidden = raw[...].astype(jnp.float32)
    factor = lax.rsqrt(jnp.mean(hidden * hidden, axis=-1, keepdims=True) + epsilon)
    xg[rows_of(me), :] = (hidden * factor * gain[...]).astype(jnp.bfloat16)
    own_pos.wait()
    own_pad.wait()
    pos_col[...] = jnp.broadcast_to(pos[...], (HEAD_DIM, n * rows)).T

    pl.semaphore_wait(
        barrier, phase_n + has_left.astype(jnp.int32) + has_right.astype(jnp.int32)
    )

    def neighbour(side):
        return lax.rem(me + 1 - 2 * side + n, n)

    def chunk_window(chunk):
        return slice(edges[chunk], edges[chunk + 1])

    def token_copy(block, side, chunk, receiver=None):
        receiver = neighbour(side) if receiver is None else receiver
        window = chunk_window(chunk)
        return pltpu.make_async_remote_copy(
            src_ref=xg.at[rows_of(block), window],
            dst_ref=xg.at[rows_of(block), window],
            send_sem=x_send,
            recv_sem=x_recv.at[block - (block > receiver).astype(jnp.int32), chunk],
            device_id={"tensor": neighbour(side)},
            device_id_type=MESH,
        )

    half = cols // 2

    def frame_copy(ref, slot, bit, last, piece, send, recv):
        target = slot + bit
        window = pl.ds(piece * half, half)
        index = target % last + target // (2 * last) * last
        place = recv.at[0] if target & last else recv.at[2 * index - 1 + piece]
        return pltpu.make_async_remote_copy(
            src_ref=ref.at[pl.ds(slot * span, span), window],
            dst_ref=ref.at[pl.ds(target * span, span), window],
            send_sem=send,
            recv_sem=place,
            device_id={"frame": flip(me_f, bit)},
            device_id_type=MESH,
        )

    def plan(ref, order, send, recv):
        steps, held = [], [0]
        last = order[-1]

        def copies(slot, onto):
            return [[frame_copy(ref, slot, bit, last, c, send, recv) for c in range(2)] for bit in onto]

        for p, bit in enumerate(order[:-1]):
            fresh = [slot + bit for slot in held]
            for slot in fresh:
                onward = copies(slot, order[p + 1:])
                for piece, arrival in enumerate(copies(slot - bit, [bit])[0]):
                    steps.append((arrival, [both[piece] for both in onward]))
            held = held + fresh
        own = [copy for both in copies(0, order) for copy in both]
        late = pl.ds(0, len(held) * span)
        rest = pltpu.make_async_remote_copy(
            src_ref=ref.at[late],
            dst_ref=ref.at[late],
            send_sem=send,
            recv_sem=recv.at[0],
            device_id={"frame": flip(me_f, last)},
            device_id_type=MESH,
        )
        return own, steps, rest

    k_own, k_steps, k_rest = plan(kg, k_order, k_send, k_recv)
    v_own, v_steps, v_rest = plan(vg, v_order, v_send, v_recv)
    for pair in zip(k_own, v_own):
        for copy in pair:
            copy.start()
    for chunk in range(n_x):
        @pl.when(has_right)
        def _():
            token_copy(me, 0, chunk).start()

        @pl.when(has_left)
        def _():
            token_copy(me, 1, chunk).start()

    relays = list(zip(k_steps, v_steps))
    cuts = [0] + [len(relays) * (i + 1) // (n_x + 2) for i in range(n_x)] + [len(relays)]

    def frame_steps(turn):
        for pair in relays[cuts[turn]:cuts[turn + 1]]:
            for arrival, onward in pair:
                arrival.wait_recv()
                for copy in onward:
                    copy.start()

    def frames_done():
        k_rest.wait_recv()
        v_rest.wait_recv()

    slot_of = lax.broadcasted_iota(jnp.int32, (1, span), 1)
    pieces = []
    for slot in range(frames_n):
        owner = me_f
        for bit in bits:
            if slot & bit:
                owner = flip(owner, bit)
        pieces.append(slot_of + owner * span)
    frame_index = jnp.concatenate(pieces, axis=1)
    visible_frames = frame_index < frames_n * span - pad[...]

    scale = HEAD_DIM ** (-0.5)

    def q_step(block, count, place, chunk):
        window = chunk_window(chunk)
        at = rows_of(block, count)
        held = rows_of(place, count)
        product = jnp.dot(xg[at, window], wq[window, :], preferred_element_type=jnp.float32)
        if chunk > 0:
            product = qacc[held, :] + product
        if chunk < n_x - 1:
            qacc[held, :] = product
        else:
            qall[at, :] = (product * scale).astype(jnp.bfloat16)

    def attend(block, count):
        at = rows_of(block, count)
        visible = (frame_index <= pos_col[at, :1]) & visible_frames
        windows = [slice(i, i + HEAD_DIM) for i in range(0, cols, HEAD_DIM)]
        scores = [
            lax.dot_general(
                qall[at, window], kg[:, window], (((1,), (1,)), ((), ())),
                preferred_element_type=jnp.float32,
            )
            for window in windows
        ]
        scores = [jnp.where(visible, score, masked_score) for score in scores]
        highest = [jnp.max(score, axis=-1, keepdims=True) for score in scores]
        weights = [jnp.exp(score - top) for score, top in zip(scores, highest)]
        totals = [jnp.sum(weight, axis=-1, keepdims=True) for weight in weights]
        gathered = [
            jnp.dot(weight.astype(jnp.bfloat16), vg[:, window], preferred_element_type=jnp.float32)
            for weight, window in zip(weights, windows)
        ]
        for window, value, total in zip(windows, gathered, totals):
            abuf[at, window] = (value / total).astype(jnp.bfloat16)

    def part_window(tile):
        return pl.ds(pl.multiple_of(tile * p_tile, p_tile), p_tile)

    def whole_slot(receiver):
        inner = jnp.where(2 * receiver < n, 0, 1)
        return jnp.where(receiver == 0, 1, jnp.where(receiver == n - 1, 0, inner))

    def whole_wait():
        slot = whole_slot(me)
        pltpu.make_async_remote_copy(
            src_ref=pbuf.at[rows_of(me)],
            dst_ref=rbuf.at[slot, rows_of(me)],
            send_sem=p_send,
            recv_sem=p_recv.at[n * n_part],
            device_id={"tensor": neighbour(0)},
            device_id_type=MESH,
        ).wait_recv()

    def part_move(block, side, tile, far, receiver):
        slot = jnp.where(far, 1 - side, side)
        towards = jnp.where(far, block, neighbour(side))
        receiver = towards if receiver is None else receiver
        whole = (block == receiver) & (slot == whole_slot(receiver))
        return pltpu.make_async_remote_copy(
            src_ref=pbuf.at[rows_of(block), part_window(tile)],
            dst_ref=rbuf.at[slot, rows_of(block), part_window(tile)],
            send_sem=p_send,
            recv_sem=p_recv.at[jnp.where(whole, n * n_part, block * n_part + tile)],
            device_id={"tensor": towards},
            device_id_type=MESH,
        )

    def part_copy(block, side, tile, far=False):
        return part_move(block, side, tile, far, None)

    def part_here(block, side, tile):
        return part_move(block, side, tile, False, me)

    def project(block, count, first_tile, send):
        at = rows_of(block, count)

        def body(index, _):
            tile = lax.rem(index + first_tile, n_out)
            window = pl.ds(pl.multiple_of(tile * o_tile, o_tile), o_tile)
            pbuf[at, window] = jnp.dot(
                abuf[at, :], wo[:, window], preferred_element_type=jnp.float32
            ).astype(jnp.bfloat16)

            if send is not None:
                send(tile)
            return 0

        lax.fori_loop(0, n_out, body, 0)

    def add_part(block, side, tile):
        at = rows_of(block)
        window = part_window(tile)
        part_here(block, side, tile).wait_recv()
        pbuf[at, window] = (
            pbuf[at, window].astype(jnp.float32) + rbuf[side, at, window].astype(jnp.float32)
        ).astype(jnp.bfloat16)

    def parts_of(tile):
        return [tile * per_out + part for part in range(per_out)]

    def drain_inputs():
        def drain_tokens(count):
            sent = pl.ds(0, count * rows)
            pltpu.make_async_remote_copy(
                src_ref=xg.at[sent],
                dst_ref=xg.at[sent],
                send_sem=x_send,
                recv_sem=x_recv.at[0, 0],
                device_id={"tensor": neighbour(0)},
                device_id_type=MESH,
            ).wait_send()

        @pl.when(middle)
        def _():
            drain_tokens(n + 1)

        @pl.when(jnp.logical_not(middle))
        def _():
            drain_tokens(1)

        others = pl.ds(0, (frames_n - 1) * span)
        for ref, send, recv in ((kg, k_send, k_recv), (vg, v_send, v_recv)):
            pltpu.make_async_remote_copy(
                src_ref=ref.at[others],
                dst_ref=ref.at[others],
                send_sem=send,
                recv_sem=recv.at[0],
                device_id={"frame": flip(me_f, bits[0])},
                device_id_type=MESH,
            ).wait_send()

    @pl.when(jnp.logical_not(middle))
    def _():
        heading = jnp.where(has_left, -1, 1)
        arriving = jnp.where(has_left, 0, 1)
        leaving = 1 - arriving
        near = me + heading
        first = jnp.minimum(me, near)
        frame_steps(0)
        q_load.wait()
        for chunk in range(n_x):
            token_copy(near, arriving, chunk, me).wait_recv()
            q_step(first, 2, 0, chunk)
            frame_steps(chunk + 1)
        frames_done()
        attend(near, 1)
        o_load.wait()

        def send_near(tile):
            for part in parts_of(tile):
                @pl.when(part < n_part - defer)
                def _():
                    part_copy(near, leaving, part).start()

        project(near, 1, 0, send_near)

        def stage_body(stage, _):
            block = me + heading * stage

            for chunk in range(n_x):
                token_copy(block, arriving, chunk, me).wait_recv()
                q_step(block, 1, 0, chunk)
            attend(block, 1)

            def send_block(tile):
                for part in parts_of(tile):
                    far = jnp.logical_and(stage == n - 1, part >= chained)

                    @pl.when(far & has_left & (part >= alone))
                    def _():
                        add_part(block, 0, part)

                    part_copy(block, leaving, part, far).start()

            project(block, 1, 0, send_block)
            return 0

        lax.fori_loop(2, n, stage_body, 0)
        for part in range(n_part - defer, n_part):
            part_copy(near, leaving, part).start()
        attend(me, 1)
        project(me, 1, 0, None)
        drain_inputs()

        whole_wait()

        def sum_body(tile, _):
            window = part_window(tile)
            total = pbuf[rows_of(me), window].astype(jnp.float32)
            total = total + rbuf[arriving, rows_of(me), window].astype(jnp.float32)

            @pl.when(tile < chained)
            def _():
                out[:, window] = total.astype(jnp.bfloat16)

            @pl.when(tile >= chained)
            def _():
                part_here(me, leaving, tile).wait_recv()
                straight = rbuf[leaving, rows_of(me), window].astype(jnp.float32)
                out[:, window] = (total + straight).astype(jnp.bfloat16)

            return 0

        def sum_index(index, _):
            return sum_body(lax.rem(index + chained, n_part), 0)

        lax.fori_loop(0, n_part, sum_index, 0)

    @pl.when(middle)
    def _():
        frame_steps(0)
        q_load.wait()
        for chunk in range(n_x):
            for side, block in ((0, me - 1), (1, me + 1)):
                token_copy(block, side, chunk, me).wait_recv()
                token_copy(block, side, chunk).start()
            q_step(me - 1, 3, 0, chunk)
            frame_steps(chunk + 1)

        def near_attend():
            frames_done()
            attend(me - 1, 3)

        def stage_body(stage, _):
            for chunk in range(n_x):
                def side_body(side, _):
                    block = me - stage + 2 * side * stage

                    @pl.when(jnp.logical_and(block >= 0, block < n))
                    def _():
                        token_copy(block, side, chunk, me).wait_recv()
                        token_copy(block, side, chunk).start()
                        q_step(block, 1, side, chunk)

                    return 0

                lax.fori_loop(0, 2, side_body, 0)
                if chunk == 0:
                    pl.when(stage == 2)(near_attend)

            def attend_body(side, _):
                block = me - stage + 2 * side * stage

                @pl.when(jnp.logical_and(block >= 0, block < n))
                def _():
                    attend(block, 1)

                return 0

            lax.fori_loop(0, 2, attend_body, 0)
            return 0

        if n == 3:
            near_attend()
        lax.fori_loop(2, n - 1, stage_body, 0)
        groups = max(1, n * rows // HEAD_DIM)
        while n % groups:
            groups -= 1
        count = n // groups
        o_load.wait()

        def group_body(group, _):
            def send_started(tile):
                last = group == groups - 1
                for part in parts_of(tile):
                    @pl.when((me == 1) & last & (part >= chained))
                    def _():
                        part_copy(n - 1, 0, part).start()


                    @pl.when((me == n - 2) & (group == 0) & (part >= chained) & (part < alone))
                    def _():
                        part_copy(0, 1, part).start()

            project(group * count, count, chained // per_out % n_out, send_started)
            return 0

        lax.fori_loop(0, groups, group_body, 0)

        @pl.when(me == n - 2)
        def _():
            for part in range(alone, n_part):
                part_copy(0, 0, part).start()

        @pl.when(me == n - 3)
        def _():
            for part in range(alone, n_part):
                part_copy(0, 1, part).start()

        def relay(block, side, tile):
            add_part(block, side, tile)
            part_copy(block, side, tile).start()

        def relay_body(index, _):
            def side_body(turn, _):
                side = jnp.where(low_half, turn, 1 - turn)
                at = index - turn * lag
                stage = 1 + lax.div(jnp.maximum(at, 0), n_part)
                tile = lax.rem(jnp.maximum(at, 0), n_part)
                block = jnp.where(side == 0, stage, n - 1 - stage)
                passes = jnp.where(side == 0, block > me, block < me)
                chain = (stage < n - 1) | ((stage == n - 1) & (tile < chained))

                @pl.when((at >= 0) & chain & passes)
                def _():
                    relay(block, side, tile)

                far = index - (n - 3) * n_part - early
                carried = chained + far >= alone
                beside = jnp.where(side == 0, me == 1, (me == n - 2) | (carried & (me == n - 3)))

                @pl.when((far >= 0) & (far < direct) & jnp.logical_not(beside))
                def _():
                    relay(jnp.where(side == 0, n - 1, 0), side, chained + far)

                return 0

            lax.fori_loop(0, 2, side_body, 0)
            return 0

        behind = jnp.minimum(me, n - 1 - me) * n_part
        lax.fori_loop(jnp.minimum(behind, (n - 3) * n_part + early), (n - 1) * n_part + lag, relay_body, 0)

        whole_wait()
        slot = whole_slot(me)

        def sum_body(tile, _):
            window = part_window(tile)
            part_here(me, 1 - slot, tile).wait_recv()
            total = pbuf[rows_of(me), window].astype(jnp.float32)
            for side in range(2):
                total = total + rbuf[side, rows_of(me), window].astype(jnp.float32)
            out[:, window] = total.astype(jnp.bfloat16)
            return 0

        lax.fori_loop(0, n_part, sum_body, 0)
        drain_inputs()

    others = pl.ds(0, (n - 1) * rows)
    pltpu.make_async_remote_copy(
        src_ref=pbuf.at[others],
        dst_ref=rbuf.at[0, others],
        send_sem=p_send,
        recv_sem=p_recv.at[0],
        device_id={"tensor": neighbour(0)},
        device_id_type=MESH,
    ).wait_send()


def divisor(total, most):
    return math.gcd(total, most)


def per_device(
    n, frames_n,
    tokens, norm_gain, query_weight, out_weight, cache_keys, cache_values, token_pos, frame_pad
):
    rows, seqs, width = tokens.shape
    cols = query_weight.shape[1]
    span = cache_keys.shape[0]
    unit = divisor(width, 256)
    shares = (5, 5, 4, 2)
    edges = [width // unit * sum(shares[:i]) // sum(shares) * unit for i in range(len(shares) + 1)]
    o_tile = divisor(width, 512)
    p_tile = divisor(o_tile, 512)
    n_x = len(shares)
    n_part = width // p_tile
    lag = max(1, 5 * n_part // 8)
    direct = n_part if n > 2 else 0
    early = -(2 * n_part // 8)
    carry = 3 * n_part // 8 if n > 3 else 0
    defer = n_part // 4 if n > 3 else 0
    hbm = pl.BlockSpec(memory_space=pltpu.HBM)
    vmem = pl.BlockSpec(memory_space=pltpu.VMEM)
    bf16 = jnp.bfloat16
    dma = pltpu.SemaphoreType.DMA
    result = pl.pallas_call(
        functools.partial(kernel, n, frames_n, edges, o_tile, p_tile, lag, direct, early, carry, defer),
        out_shape=pltpu.VMEM((rows, width), bf16),
        in_specs=[hbm] * 8,
        out_specs=vmem,
        scratch_shapes=[
            pltpu.VMEM(query_weight.shape, bf16),
            pltpu.VMEM(out_weight.shape, bf16),
            pltpu.VMEM((frames_n * span, cols), bf16),
            pltpu.VMEM((frames_n * span, cols), bf16),
            pltpu.VMEM((n * rows, HEAD_DIM), jnp.int32),
            pltpu.VMEM((1, width), jnp.float32),
            pltpu.VMEM((1, n * rows), jnp.int32),
            pltpu.VMEM((1, 1), jnp.int32),
            pltpu.VMEM((rows, width), bf16),
            pltpu.VMEM(((n + 1) * rows, width), bf16),
            pltpu.VMEM((3 * rows, cols), jnp.float32),
            pltpu.VMEM((n * rows, cols), bf16),
            pltpu.VMEM((n * rows, cols), bf16),
            pltpu.VMEM((n * rows, width), bf16),
            pltpu.VMEM((2, n * rows, width), bf16),
            dma((2,)),
            dma(()),
            dma((3,)),
            dma((2,)),
            dma(()),
            dma((frames_n - 1,)),
            dma(()),
            dma((frames_n - 1,)),
            dma(()),
            dma((n - 1, n_x)),
            dma(()),
            dma((n * n_part + 1,)),
        ],
        compiler_params=pltpu.CompilerParams(collective_id=0, has_side_effects=True),
    )(
        tokens.reshape(rows, width),
        norm_gain.reshape(1, width),
        query_weight,
        out_weight,
        cache_keys.reshape(span, cols),
        cache_values.reshape(span, cols),
        token_pos.reshape(1, n * rows),
        frame_pad.reshape(1, 1),
    )
    return result.reshape(rows, seqs, width)


def solution(mesh):
    placed = (
        P(("frame", "tensor"), None, None),
        P(),
        P(None, "tensor"),
        P("tensor", None),
        P("frame", None, "tensor"),
        P("frame", None, "tensor"),
        P("frame", None),
        P(),
    )
    return jax.shard_map(
        functools.partial(per_device, mesh.shape["tensor"], mesh.shape["frame"]),
        mesh=mesh,
        in_specs=placed,
        out_specs=P(("frame", "tensor"), None, None),
        check_vma=False,
    )
```

```python
import functools
import math

import jax
import jax.numpy as jnp
from jax import lax
from jax.experimental import pallas as pl
from jax.experimental.pallas import tpu as pltpu
from jax.sharding import PartitionSpec as P

HEAD_DIM = 128
epsilon = 1e-06
masked_score = -1e30
MESH = pl.DeviceIdType.MESH


def flip(index, bit):
    return index + bit - 2 * bit * lax.rem(lax.div(index, bit), 2)


def kernel(
    n, frames_n, edges, o_tile, p_tile, lag, direct, early, carry, defer,
    tok, gain_hbm, wq_hbm, wo_hbm, keys, values, pos_hbm, pad_hbm,
    out,
    wq, wo, kg, vg, pos_col, gain, pos, pad, raw, xg, qacc, qall, abuf, pbuf, rbuf,
    weight_sem, own_sem, small_sem, kv_own, k_send, k_recv, v_send, v_recv,
    x_send, x_recv, p_send, p_recv,
):
    me_f = lax.axis_index("frame")
    me = lax.axis_index("tensor")
    rows = tok.shape[0]
    width = tok.shape[1]
    cols = wq.shape[1]
    span = keys.shape[0]
    bits = [1 << b for b in range(int(math.log2(frames_n)))][::-1]
    phase_n = len(bits)
    k_order = bits
    v_order = bits[1::-1] + bits[2:] if phase_n > 1 else bits
    n_x = len(edges) - 1
    n_out = width // o_tile
    n_part = width // p_tile
    per_out = o_tile // p_tile
    chained = n_part - direct
    alone = n_part - carry
    has_left = me > 0
    has_right = me < n - 1
    middle = jnp.logical_and(has_left, has_right)
    low_half = 2 * me < n

    q_load = pltpu.make_async_copy(wq_hbm, wq, weight_sem.at[0])
    o_load = pltpu.make_async_copy(wo_hbm, wo, weight_sem.at[1])

    def rows_of(block, count=1):
        return pl.ds(pl.multiple_of(block * rows, rows), count * rows)

    own_x = pltpu.make_async_copy(tok, raw, own_sem)
    own_gain = pltpu.make_async_copy(gain_hbm, gain, small_sem.at[0])
    own_pos = pltpu.make_async_copy(pos_hbm, pos, small_sem.at[1])
    own_pad = pltpu.make_async_copy(pad_hbm, pad, small_sem.at[2])
    own_k = pltpu.make_async_copy(keys, kg.at[pl.ds(0, span)], kv_own.at[0])
    own_v = pltpu.make_async_copy(values, vg.at[pl.ds(0, span)], kv_own.at[1])

    barrier = pltpu.get_barrier_semaphore()
    for bit in bits:
        pl.semaphore_signal(
            barrier, inc=1, device_id={"frame": flip(me_f, bit)}, device_id_type=MESH
        )

    @pl.when(has_left)
    def _():
        pl.semaphore_signal(barrier, inc=1, device_id={"tensor": me - 1}, device_id_type=MESH)

    @pl.when(has_right)
    def _():
        pl.semaphore_signal(barrier, inc=1, device_id={"tensor": me + 1}, device_id_type=MESH)

    own_x.start()
    own_gain.start()
    own_pos.start()
    own_pad.start()
    own_k.start()
    own_v.start()

    own_x.wait()
    own_gain.wait()
    own_k.wait()
    own_v.wait()
    q_load.start()
    o_load.start()
    hidden = raw[...].astype(jnp.float32)
    factor = lax.rsqrt(jnp.mean(hidden * hidden, axis=-1, keepdims=True) + epsilon)
    xg[rows_of(me), :] = (hidden * factor * gain[...]).astype(jnp.bfloat16)
    own_pos.wait()
    own_pad.wait()
    pos_col[...] = jnp.broadcast_to(pos[...], (HEAD_DIM, n * rows)).T

    pl.semaphore_wait(
        barrier, phase_n + has_left.astype(jnp.int32) + has_right.astype(jnp.int32)
    )

    def neighbour(side):
        return lax.rem(me + 1 - 2 * side + n, n)

    def chunk_window(chunk):
        return slice(edges[chunk], edges[chunk + 1])

    def token_copy(block, side, chunk, receiver=None):
        receiver = neighbour(side) if receiver is None else receiver
        window = chunk_window(chunk)
        return pltpu.make_async_remote_copy(
            src_ref=xg.at[rows_of(block), window],
            dst_ref=xg.at[rows_of(block), window],
            send_sem=x_send,
            recv_sem=x_recv.at[block - (block > receiver).astype(jnp.int32), chunk],
            device_id={"tensor": neighbour(side)},
            device_id_type=MESH,
        )

    half = cols // 2

    def frame_copy(ref, slot, bit, last, piece, send, recv):
        target = slot + bit
        window = pl.ds(piece * half, half)
        index = target % last + target // (2 * last) * last
        place = recv.at[0] if target & last else recv.at[2 * index - 1 + piece]
        return pltpu.make_async_remote_copy(
            src_ref=ref.at[pl.ds(slot * span, span), window],
            dst_ref=ref.at[pl.ds(target * span, span), window],
            send_sem=send,
            recv_sem=place,
            device_id={"frame": flip(me_f, bit)},
            device_id_type=MESH,
        )

    def plan(ref, order, send, recv):
        steps, held = [], [0]
        last = order[-1]

        def copies(slot, onto):
            return [[frame_copy(ref, slot, bit, last, c, send, recv) for c in range(2)] for bit in onto]

        for p, bit in enumerate(order[:-1]):
            fresh = [slot + bit for slot in held]
            for slot in fresh:
                onward = copies(slot, order[p + 1:])
                for piece, arrival in enumerate(copies(slot - bit, [bit])[0]):
                    steps.append((arrival, [both[piece] for both in onward]))
            held = held + fresh
        own = [copy for both in copies(0, order) for copy in both]
        late = pl.ds(0, len(held) * span)
        rest = pltpu.make_async_remote_copy(
            src_ref=ref.at[late],
            dst_ref=ref.at[late],
            send_sem=send,
            recv_sem=recv.at[0],
            device_id={"frame": flip(me_f, last)},
            device_id_type=MESH,
        )
        return own, steps, rest

    k_own, k_steps, k_rest = plan(kg, k_order, k_send, k_recv)
    v_own, v_steps, v_rest = plan(vg, v_order, v_send, v_recv)
    for pair in zip(k_own, v_own):
        for copy in pair:
            copy.start()
    for chunk in range(n_x):
        @pl.when(has_right)
        def _():
            token_copy(me, 0, chunk).start()

        @pl.when(has_left)
        def _():
            token_copy(me, 1, chunk).start()

    relays = list(zip(k_steps, v_steps))
    cuts = [0] + [len(relays) * (i + 1) // (n_x + 2) for i in range(n_x)] + [len(relays)]

    def frame_steps(turn):
        for pair in relays[cuts[turn]:cuts[turn + 1]]:
            for arrival, onward in pair:
                arrival.wait_recv()
                for copy in onward:
                    copy.start()

    def frames_done():
        k_rest.wait_recv()
        v_rest.wait_recv()

    slot_of = lax.broadcasted_iota(jnp.int32, (1, span), 1)
    pieces = []
    for slot in range(frames_n):
        owner = me_f
        for bit in bits:
            if slot & bit:
                owner = flip(owner, bit)
        pieces.append(slot_of + owner * span)
    frame_index = jnp.concatenate(pieces, axis=1)
    visible_frames = frame_index < frames_n * span - pad[...]

    scale = HEAD_DIM ** (-0.5)

    def q_step(block, count, place, chunk):
        window = chunk_window(chunk)
        at = rows_of(block, count)
        held = rows_of(place, count)
        product = jnp.dot(xg[at, window], wq[window, :], preferred_element_type=jnp.float32)
        if chunk > 0:
            product = qacc[held, :] + product
        if chunk < n_x - 1:
            qacc[held, :] = product
        else:
            qall[at, :] = (product * scale).astype(jnp.bfloat16)

    def attend(block, count):
        at = rows_of(block, count)
        visible = (frame_index <= pos_col[at, :1]) & visible_frames
        windows = [slice(i, i + HEAD_DIM) for i in range(0, cols, HEAD_DIM)]
        scores = [
            lax.dot_general(
                qall[at, window], kg[:, window], (((1,), (1,)), ((), ())),
                preferred_element_type=jnp.float32,
            )
            for window in windows
        ]
        scores = [jnp.where(visible, score, masked_score) for score in scores]
        highest = [jnp.max(score, axis=-1, keepdims=True) for score in scores]
        weights = [jnp.exp(score - top) for score, top in zip(scores, highest)]
        totals = [jnp.sum(weight, axis=-1, keepdims=True) for weight in weights]
        gathered = [
            jnp.dot(weight.astype(jnp.bfloat16), vg[:, window], preferred_element_type=jnp.float32)
            for weight, window in zip(weights, windows)
        ]
        for window, value, total in zip(windows, gathered, totals):
            abuf[at, window] = (value / total).astype(jnp.bfloat16)

    def part_window(tile):
        return pl.ds(pl.multiple_of(tile * p_tile, p_tile), p_tile)

    def whole_slot(receiver):
        inner = jnp.where(2 * receiver < n, 0, 1)
        return jnp.where(receiver == 0, 1, jnp.where(receiver == n - 1, 0, inner))

    def whole_wait():
        slot = whole_slot(me)
        pltpu.make_async_remote_copy(
            src_ref=pbuf.at[rows_of(me)],
            dst_ref=rbuf.at[slot, rows_of(me)],
            send_sem=p_send,
            recv_sem=p_recv.at[n * n_part],
            device_id={"tensor": neighbour(0)},
            device_id_type=MESH,
        ).wait_recv()

    def part_move(block, side, tile, far, receiver):
        slot = jnp.where(far, 1 - side, side)
        towards = jnp.where(far, block, neighbour(side))
        receiver = towards if receiver is None else receiver
        whole = (block == receiver) & (slot == whole_slot(receiver))
        return pltpu.make_async_remote_copy(
            src_ref=pbuf.at[rows_of(block), part_window(tile)],
            dst_ref=rbuf.at[slot, rows_of(block), part_window(tile)],
            send_sem=p_send,
            recv_sem=p_recv.at[jnp.where(whole, n * n_part, block * n_part + tile)],
            device_id={"tensor": towards},
            device_id_type=MESH,
        )

    def part_copy(block, side, tile, far=False):
        return part_move(block, side, tile, far, None)

    def part_here(block, side, tile):
        return part_move(block, side, tile, False, me)

    def project(block, count, first_tile, send):
        at = rows_of(block, count)

        def body(index, _):
            tile = lax.rem(index + first_tile, n_out)
            window = pl.ds(pl.multiple_of(tile * o_tile, o_tile), o_tile)
            pbuf[at, window] = jnp.dot(
                abuf[at, :], wo[:, window], preferred_element_type=jnp.float32
            ).astype(jnp.bfloat16)

            if send is not None:
                send(tile)
            return 0

        lax.fori_loop(0, n_out, body, 0)

    def add_part(block, side, tile):
        at = rows_of(block)
        window = part_window(tile)
        part_here(block, side, tile).wait_recv()
        pbuf[at, window] = (
            pbuf[at, window].astype(jnp.float32) + rbuf[side, at, window].astype(jnp.float32)
        ).astype(jnp.bfloat16)

    def parts_of(tile):
        return [tile * per_out + part for part in range(per_out)]

    def drain_inputs():
        def drain_tokens(count):
            sent = pl.ds(0, count * rows)
            pltpu.make_async_remote_copy(
                src_ref=xg.at[sent],
                dst_ref=xg.at[sent],
                send_sem=x_send,
                recv_sem=x_recv.at[0, 0],
                device_id={"tensor": neighbour(0)},
                device_id_type=MESH,
            ).wait_send()

        @pl.when(middle)
        def _():
            drain_tokens(n + 1)

        @pl.when(jnp.logical_not(middle))
        def _():
            drain_tokens(1)

        others = pl.ds(0, (frames_n - 1) * span)
        for ref, send, recv in ((kg, k_send, k_recv), (vg, v_send, v_recv)):
            pltpu.make_async_remote_copy(
                src_ref=ref.at[others],
                dst_ref=ref.at[others],
                send_sem=send,
                recv_sem=recv.at[0],
                device_id={"frame": flip(me_f, bits[0])},
                device_id_type=MESH,
            ).wait_send()

    @pl.when(jnp.logical_not(middle))
    def _():
        heading = jnp.where(has_left, -1, 1)
        arriving = jnp.where(has_left, 0, 1)
        leaving = 1 - arriving
        near = me + heading
        first = jnp.minimum(me, near)
        frame_steps(0)
        q_load.wait()
        for chunk in range(n_x):
            token_copy(near, arriving, chunk, me).wait_recv()
            q_step(first, 2, 0, chunk)
            frame_steps(chunk + 1)
        frames_done()
        attend(near, 1)
        o_load.wait()

        def send_near(tile):
            for part in parts_of(tile):
                @pl.when(part < n_part - defer)
                def _():
                    part_copy(near, leaving, part).start()

        project(near, 1, 0, send_near)

        def stage_body(stage, _):
            block = me + heading * stage

            for chunk in range(n_x):
                token_copy(block, arriving, chunk, me).wait_recv()
                q_step(block, 1, 0, chunk)
            attend(block, 1)

            def send_block(tile):
                for part in parts_of(tile):
                    far = jnp.logical_and(stage == n - 1, part >= chained)

                    @pl.when(far & has_left & (part >= alone))
                    def _():
                        add_part(block, 0, part)

                    part_copy(block, leaving, part, far).start()

            project(block, 1, 0, send_block)
            return 0

        lax.fori_loop(2, n, stage_body, 0)
        for part in range(n_part - defer, n_part):
            part_copy(near, leaving, part).start()
        attend(me, 1)
        project(me, 1, 0, None)
        drain_inputs()

        whole_wait()

        def sum_body(tile, _):
            window = part_window(tile)
            total = pbuf[rows_of(me), window].astype(jnp.float32)
            total = total + rbuf[arriving, rows_of(me), window].astype(jnp.float32)

            @pl.when(tile < chained)
            def _():
                out[:, window] = total.astype(jnp.bfloat16)

            @pl.when(tile >= chained)
            def _():
                part_here(me, leaving, tile).wait_recv()
                straight = rbuf[leaving, rows_of(me), window].astype(jnp.float32)
                out[:, window] = (total + straight).astype(jnp.bfloat16)

            return 0

        def sum_index(index, _):
            return sum_body(lax.rem(index + chained, n_part), 0)

        lax.fori_loop(0, n_part, sum_index, 0)

    @pl.when(middle)
    def _():
        frame_steps(0)
        q_load.wait()
        for chunk in range(n_x):
            for side, block in ((0, me - 1), (1, me + 1)):
                token_copy(block, side, chunk, me).wait_recv()
                token_copy(block, side, chunk).start()
            q_step(me - 1, 3, 0, chunk)
            frame_steps(chunk + 1)

        def near_attend():
            frames_done()
            attend(me - 1, 3)

        def stage_body(stage, _):
            for chunk in range(n_x):
                def side_body(side, _):
                    block = me - stage + 2 * side * stage

                    @pl.when(jnp.logical_and(block >= 0, block < n))
                    def _():
                        token_copy(block, side, chunk, me).wait_recv()
                        token_copy(block, side, chunk).start()
                        q_step(block, 1, side, chunk)

                    return 0

                lax.fori_loop(0, 2, side_body, 0)
                if chunk == 0:
                    pl.when(stage == 2)(near_attend)

            def attend_body(side, _):
                block = me - stage + 2 * side * stage

                @pl.when(jnp.logical_and(block >= 0, block < n))
                def _():
                    attend(block, 1)

                return 0

            lax.fori_loop(0, 2, attend_body, 0)
            return 0

        if n == 3:
            near_attend()
        lax.fori_loop(2, n - 1, stage_body, 0)
        groups = max(1, n * rows // HEAD_DIM)
        while n % groups:
            groups -= 1
        count = n // groups
        o_load.wait()

        def group_body(group, _):
            def send_started(tile):
                last = group == groups - 1
                for part in parts_of(tile):
                    @pl.when((me == 1) & last & (part >= chained))
                    def _():
                        part_copy(n - 1, 0, part).start()


                    @pl.when((me == n - 2) & (group == 0) & (part >= chained) & (part < alone))
                    def _():
                        part_copy(0, 1, part).start()

            project(group * count, count, chained // per_out % n_out, send_started)
            return 0

        lax.fori_loop(0, groups, group_body, 0)

        @pl.when(me == n - 2)
        def _():
            for part in range(alone, n_part):
                part_copy(0, 0, part).start()

        @pl.when(me == n - 3)
        def _():
            for part in range(alone, n_part):
                part_copy(0, 1, part).start()

        def relay(block, side, tile):
            add_part(block, side, tile)
            part_copy(block, side, tile).start()

        def relay_body(index, _):
            def side_body(turn, _):
                side = jnp.where(low_half, turn, 1 - turn)
                at = index - turn * lag
                stage = 1 + lax.div(jnp.maximum(at, 0), n_part)
                tile = lax.rem(jnp.maximum(at, 0), n_part)
                block = jnp.where(side == 0, stage, n - 1 - stage)
                passes = jnp.where(side == 0, block > me, block < me)
                chain = (stage < n - 1) | ((stage == n - 1) & (tile < chained))

                @pl.when((at >= 0) & chain & passes)
                def _():
                    relay(block, side, tile)

                far = index - (n - 3) * n_part - early
                carried = chained + far >= alone
                beside = jnp.where(side == 0, me == 1, (me == n - 2) | (carried & (me == n - 3)))

                @pl.when((far >= 0) & (far < direct) & jnp.logical_not(beside))
                def _():
                    relay(jnp.where(side == 0, n - 1, 0), side, chained + far)

                return 0

            lax.fori_loop(0, 2, side_body, 0)
            return 0

        behind = jnp.minimum(me, n - 1 - me) * n_part
        lax.fori_loop(jnp.minimum(behind, (n - 3) * n_part + early), (n - 1) * n_part + lag, relay_body, 0)

        whole_wait()
        slot = whole_slot(me)

        def sum_body(tile, _):
            window = part_window(tile)
            part_here(me, 1 - slot, tile).wait_recv()
            total = pbuf[rows_of(me), window].astype(jnp.float32)
            for side in range(2):
                total = total + rbuf[side, rows_of(me), window].astype(jnp.float32)
            out[:, window] = total.astype(jnp.bfloat16)
            return 0

        lax.fori_loop(0, n_part, sum_body, 0)
        drain_inputs()

    others = pl.ds(0, (n - 1) * rows)
    pltpu.make_async_remote_copy(
        src_ref=pbuf.at[others],
        dst_ref=rbuf.at[0, others],
        send_sem=p_send,
        recv_sem=p_recv.at[0],
        device_id={"tensor": neighbour(0)},
        device_id_type=MESH,
    ).wait_send()


def divisor(total, most):
    return math.gcd(total, most)


def per_device(
    n, frames_n,
    tokens, norm_gain, query_weight, out_weight, cache_keys, cache_values, token_pos, frame_pad
):
    rows, seqs, width = tokens.shape
    cols = query_weight.shape[1]
    span = cache_keys.shape[0]
    unit = divisor(width, 256)
    shares = (5, 5, 4, 2)
    edges = [width // unit * sum(shares[:i]) // sum(shares) * unit for i in range(len(shares) + 1)]
    o_tile = divisor(width, 512)
    p_tile = divisor(o_tile, 512)
    n_x = len(shares)
    n_part = width // p_tile
    lag = max(1, 5 * n_part // 8)
    direct = n_part if n > 2 else 0
    early = -(1 * n_part // 8)
    carry = n_part // 4 if n > 3 else 0
    defer = n_part // 4 if n > 3 else 0
    hbm = pl.BlockSpec(memory_space=pltpu.HBM)
    vmem = pl.BlockSpec(memory_space=pltpu.VMEM)
    bf16 = jnp.bfloat16
    dma = pltpu.SemaphoreType.DMA
    result = pl.pallas_call(
        functools.partial(kernel, n, frames_n, edges, o_tile, p_tile, lag, direct, early, carry, defer),
        out_shape=pltpu.VMEM((rows, width), bf16),
        in_specs=[hbm] * 8,
        out_specs=vmem,
        scratch_shapes=[
            pltpu.VMEM(query_weight.shape, bf16),
            pltpu.VMEM(out_weight.shape, bf16),
            pltpu.VMEM((frames_n * span, cols), bf16),
            pltpu.VMEM((frames_n * span, cols), bf16),
            pltpu.VMEM((n * rows, HEAD_DIM), jnp.int32),
            pltpu.VMEM((1, width), jnp.float32),
            pltpu.VMEM((1, n * rows), jnp.int32),
            pltpu.VMEM((1, 1), jnp.int32),
            pltpu.VMEM((rows, width), bf16),
            pltpu.VMEM(((n + 1) * rows, width), bf16),
            pltpu.VMEM((3 * rows, cols), jnp.float32),
            pltpu.VMEM((n * rows, cols), bf16),
            pltpu.VMEM((n * rows, cols), bf16),
            pltpu.VMEM((n * rows, width), bf16),
            pltpu.VMEM((2, n * rows, width), bf16),
            dma((2,)),
            dma(()),
            dma((3,)),
            dma((2,)),
            dma(()),
            dma((frames_n - 1,)),
            dma(()),
            dma((frames_n - 1,)),
            dma(()),
            dma((n - 1, n_x)),
            dma(()),
            dma((n * n_part + 1,)),
        ],
        compiler_params=pltpu.CompilerParams(collective_id=0, has_side_effects=True),
    )(
        tokens.reshape(rows, width),
        norm_gain.reshape(1, width),
        query_weight,
        out_weight,
        cache_keys.reshape(span, cols),
        cache_values.reshape(span, cols),
        token_pos.reshape(1, n * rows),
        frame_pad.reshape(1, 1),
    )
    return result.reshape(rows, seqs, width)


def solution(mesh):
    placed = (
        P(("frame", "tensor"), None, None),
        P(),
        P(None, "tensor"),
        P("tensor", None),
        P("frame", None, "tensor"),
        P("frame", None, "tensor"),
        P("frame", None),
        P(),
    )
    return jax.shard_map(
        functools.partial(per_device, mesh.shape["tensor"], mesh.shape["frame"]),
        mesh=mesh,
        in_specs=placed,
        out_specs=P(("frame", "tensor"), None, None),
        check_vma=False,
    )
```
